256 devices in a mesh: region: 32 (over z, y), rays: 8 (over x, core).
Axes of the slice: x: 4, y: 4, z: 8, core: 2. Of those that a mesh axis runs over, the one named last changes fastest.
Arguments:
- grid_coords: int32 [3, 32, 4, 32768], P(None, 'region', None, 'rays'), may hold values from 0 to 4095
- segment_bounds: int32 [2, 32, 32768], P(None, 'region', 'rays'), may hold values from 0 to 4, as said below
- depth_rank: int32 [32768, 32], P('rays'), may hold values from 0 to 31, each once within a row
- step_length: float32 [32, 4, 32768], P('region', None, 'rays'), may hold values from 0.01 to 0.08
- sample_depth: float32 [32, 4, 32768], P('region', None, 'rays'), may hold values from 0.5 to 4
- target_pixels: float32 [4, 32768], P(None, 'rays'), may hold values from 0 to 1.5
- weight_in: bfloat16 [32, 60, 256], P('region'), may hold values from -0.75 to 0.75
- weight_mid: bfloat16 [32, 256, 256], P('region'), may hold values from -0.375 to 0.375
- weight_out: bfloat16 [32, 4, 256], P('region'), may hold values from -0.375 to 0.375
- bias_hidden: float32 [32, 2, 256], P('region'), may hold values from -3 to 3
Outputs:
- grad_in: float32 [32, 60, 256], P('region', None, 'rays')
- grad_mid: float32 [32, 256, 256], P('region', None, 'rays')
- grad_out: float32 [32, 4, 256], P('region', None, 'rays')
- grad_bias: float32 [32, 2, 256], P('region', None, 'rays')
The draws below stay inside these ranges and needn't reach their ends.
Inputs may be any that keep to these rules, and one draw needn't show every extreme that they name: For every region and ray segment_bounds[0] <= segment_bounds[1]; the ray's live samples in the region are the slots from segment_bounds[0] to segment_bounds[1] - 1; in every region some ray has all 4 slots live.
All inputs are finite; a program needn't handle non-finite values.
Results may differ from the reference program's by a relative error of at most 0.00055.
Values sent between devices are 32-bit elements; how exact they have to be, the bound alone decides.
No kernel may reach another device: no remote copies, remote signals or barrier semaphores. Data moves between devices by JAX's collectives and lax.ppermute only.
A program may use at most 128 MiB of HBM per device.

```python
import math
import jax
import jax.numpy as jnp
from jax import lax

HID = 256
ENC = 60
GRID = 4096
SLOTS = 4
REGIONS = 32
TOTAL_RAYS = 32768


def draw_segment_bounds(key, part):
    key_capacity, key_covered, key_first = jax.random.split(key, 3)
    lowest = max(1, SLOTS // 4)
    capacity = jax.random.randint(key_capacity, (REGIONS, 1), lowest, SLOTS + 1)
    covered = jax.random.randint(key_covered, (REGIONS, TOTAL_RAYS), 0, capacity + 1)
    first_slot = jax.random.randint(key_first, (REGIONS, TOTAL_RAYS), 0, SLOTS - covered + 1)
    leading = lax.broadcasted_iota(jnp.int32, (REGIONS, TOTAL_RAYS), 1) == 0
    covered = jnp.where(leading, SLOTS, covered)
    first_slot = jnp.where(leading, 0, first_slot)
    return jnp.stack([first_slot, first_slot + covered]).astype(jnp.int32)


def touch_ends(result, stream_key, least, top_value):
    index_at = [jax.random.randint(jax.random.fold_in(stream_key, axis), (), 0, length) for axis, length in enumerate(result.shape)]
    main_axis = result.shape.index(max(result.shape))
    beside = index_at[:main_axis] + [(index_at[main_axis] + 1) % result.shape[main_axis]] + index_at[main_axis + 1:]
    return result.at[tuple(index_at)].set(least).at[tuple(beside)].set(top_value)


def steps_of(own_key, dims, cuts, least, high):
    def one(dim, shards_of):
        heights = jax.random.uniform(jax.random.fold_in(jax.random.fold_in(own_key, 6), dim), (shards_of,), jnp.float32, least / len(cuts), high / len(cuts))
        return jnp.repeat(jnp.exp(heights), dims[dim] // shards_of).reshape((-1,) + (1,) * (len(dims) - dim - 1))

    loudness = one(*cuts[0])
    for cut in cuts[1:]:
        loudness = loudness * one(*cut)
    return loudness


def scatter_about(rng, extent, width, most, cuts=(), kind=jnp.bfloat16):
    loudness = steps_of(rng, extent, cuts, -0.22, 0.18) if cuts else 1.0
    entries = jax.random.normal(rng, extent, jnp.float32) * width * loudness
    return jnp.minimum(jnp.maximum(entries, -most), most).astype(kind)


def setup_inputs(seed: int = 0) -> dict:
    key_list = jax.random.split(jax.random.key(seed), 11)
    grid_coords = touch_ends(jax.random.randint(key_list[0], (3, REGIONS, SLOTS, TOTAL_RAYS), 0, GRID), jax.random.fold_in(key_list[0], 1), 0, GRID - 1).astype(jnp.int32)
    segment_bounds = draw_segment_bounds(jax.random.fold_in(key_list[10], 71), 0)
    depth_rank = jax.vmap(lambda own: jax.random.permutation(own, REGIONS))(jax.random.split(key_list[2], TOTAL_RAYS)).reshape((TOTAL_RAYS, REGIONS)).astype(jnp.int32)
    step_length = jnp.clip(jnp.exp(math.log(0.08) - 2.0794415 * jax.random.uniform(key_list[3], (REGIONS, SLOTS, TOTAL_RAYS), jnp.float32) ** steps_of(key_list[3], (REGIONS, SLOTS, TOTAL_RAYS), ((0, 32), (2, 8)), -0.2, 0.2)), 0.01, 0.08)
    sample_depth = jnp.clip(0.5 + 3.5 * jax.random.uniform(key_list[4], (REGIONS, SLOTS, TOTAL_RAYS), jnp.float32) ** steps_of(key_list[4], (REGIONS, SLOTS, TOTAL_RAYS), ((0, 32), (2, 8)), -0.2, 0.2), 0.5, 4.0)
    target_pixels = jnp.clip(1.5 * jax.random.uniform(key_list[5], (4, TOTAL_RAYS), jnp.float32) ** steps_of(key_list[5], (4, TOTAL_RAYS), ((1, 8),), -0.2, 0.2), 0.0, 1.5)
    weight_in = scatter_about(key_list[6], (REGIONS, ENC, HID), ENC ** -0.5, 0.75, ((0, 32),))
    weight_mid = scatter_about(key_list[7], (REGIONS, HID, HID), HID ** -0.5, 0.375, ((0, 32),))
    weight_out = scatter_about(key_list[8], (REGIONS, 4, HID), HID ** -0.5, 0.375, ((0, 32),))
    bias_hidden = scatter_about(key_list[9], (REGIONS, 2, HID), 0.5, 3.0, ((0, 32),), jnp.float32)
    return {"grid_coords": grid_coords, "segment_bounds": segment_bounds, "depth_rank": depth_rank, "step_length": step_length, "sample_depth": sample_depth, "target_pixels": target_pixels, "weight_in": weight_in, "weight_mid": weight_mid, "weight_out": weight_out, "bias_hidden": bias_hidden}


depth_weight = 0.1

def encode(coords, freq_count):
    position = (coords.astype(jnp.float32) + 0.5) / GRID
    position = position.reshape(3, -1)
    scales = 2.0 ** lax.broadcasted_iota(jnp.float32, (freq_count, 1, 1), 0) * math.pi
    angle = scales * position[None]
    both = jnp.concatenate([jnp.sin(angle), jnp.cos(angle)], axis=0)
    return both.reshape(6 * freq_count, -1).astype(jnp.bfloat16)

def silu_slope(value):
    sig = jax.nn.sigmoid(value)
    return sig * (1.0 + value * (1.0 - sig))

def forward(weight_in, weight_mid, weight_out, bias_hidden, coords, bounds, step_length, sample_depth):
    slots, rays = step_length.shape
    encoded = encode(coords, weight_in.shape[0] // 6)
    contract = (((0,), (0,)), ((), ()))
    pre_one = lax.dot_general(weight_in, encoded, contract, preferred_element_type=jnp.float32) + bias_hidden[0][:, None]
    hidden_one = jax.nn.silu(pre_one).astype(jnp.bfloat16)
    pre_two = lax.dot_general(weight_mid, hidden_one, contract, preferred_element_type=jnp.float32) + bias_hidden[1][:, None]
    hidden_two = jax.nn.silu(pre_two).astype(jnp.bfloat16)
    raw_out = jnp.dot(weight_out, hidden_two, preferred_element_type=jnp.float32).reshape(4, slots, rays)
    density = jax.nn.softplus(raw_out[0])
    colour = jax.nn.sigmoid(raw_out[1:])
    slot_index = lax.broadcasted_iota(jnp.int32, (slots, rays), 0)
    live_mask = ((slot_index >= bounds[0][None]) & (slot_index < bounds[1][None])).astype(jnp.float32)
    optical = density * step_length * live_mask
    optical_before = jnp.cumsum(optical, axis=0) - optical
    blend = jnp.exp(-optical_before) * -jnp.expm1(-optical)
    segment_colour = lax.optimization_barrier(jnp.sum(blend[None] * colour, axis=1))
    segment_depth = lax.optimization_barrier(jnp.sum(blend * sample_depth, axis=0))
    log_passing = -lax.optimization_barrier(jnp.sum(optical, axis=0))
    segment = jnp.concatenate([segment_colour, segment_depth[None], log_passing[None]], axis=0)
    cache = (encoded, pre_one, hidden_one, pre_two, hidden_two, raw_out, colour, live_mask, optical, optical_before, blend)
    return (segment, cache)

def backward(weight_in, weight_mid, weight_out, step_length, sample_depth, cache, grad_segment):
    encoded, pre_one, hidden_one, pre_two, hidden_two, raw_out, colour, live_mask, optical, optical_before, blend = cache
    grad_colour = grad_segment[:3]
    usage_grad = lax.optimization_barrier(jnp.sum(grad_colour[:, None] * colour, axis=0)) + grad_segment[3][None] * sample_depth
    weighted = usage_grad * blend
    later_sum = lax.optimization_barrier(jnp.sum(weighted, axis=0))[None] - jnp.cumsum(weighted, axis=0)
    grad_optical = usage_grad * jnp.exp(-(optical_before + optical)) - later_sum - grad_segment[4][None]
    grad_density = grad_optical * step_length * live_mask * jax.nn.sigmoid(raw_out[0])
    grad_hue = grad_colour[:, None] * blend[None] * colour * (1.0 - colour)
    grad_raw = jnp.concatenate([grad_density[None], grad_hue], axis=0).reshape(4, -1).astype(jnp.bfloat16)
    contract = (((0,), (0,)), ((), ()))
    over_samples = (((1,), (1,)), ((), ()))
    grad_out = lax.dot_general(grad_raw, hidden_two, over_samples, preferred_element_type=jnp.float32)
    grad_pre_two = lax.dot_general(weight_out, grad_raw, contract, preferred_element_type=jnp.float32) * silu_slope(pre_two)
    rounded_two = grad_pre_two.astype(jnp.bfloat16)
    grad_mid = lax.dot_general(hidden_one, rounded_two, over_samples, preferred_element_type=jnp.float32)
    grad_pre_one = jnp.dot(weight_mid, rounded_two, preferred_element_type=jnp.float32) * silu_slope(pre_one)
    rounded_one = grad_pre_one.astype(jnp.bfloat16)
    grad_in = lax.dot_general(encoded, rounded_one, over_samples, preferred_element_type=jnp.float32)
    grad_bias = jnp.stack([lax.optimization_barrier(jnp.sum(grad_pre_one, axis=1)), lax.optimization_barrier(jnp.sum(grad_pre_two, axis=1))])
    return (grad_in, grad_mid, grad_out, grad_bias)

def join_segments(segments, depth_ranks, target, loss_scale):
    log_passing = segments[4]
    light_before = lax.map(lambda rank_row: jnp.exp(lax.optimization_barrier(jnp.sum(jnp.where(depth_ranks < rank_row[None], log_passing, 0.0), axis=0))), depth_ranks)
    composite_vals = lax.optimization_barrier(jnp.sum(light_before[None] * segments[:4], axis=1))
    gains = jnp.array([1.0, 1.0, 1.0, depth_weight], jnp.float32)
    grad_composite = 2.0 * loss_scale * gains[:, None] * (composite_vals - target)
    light_terms = light_before * lax.optimization_barrier(jnp.sum(grad_composite[:, None] * segments[:4], axis=0))
    later_terms = lax.map(lambda rank_row: lax.optimization_barrier(jnp.sum(jnp.where(depth_ranks > rank_row[None], light_terms, 0.0), axis=0)), depth_ranks)
    return jnp.concatenate([light_before[None] * grad_composite[:, None], later_terms[None]], axis=0)

def reference(grid_coords, segment_bounds, depth_rank, step_length, sample_depth, target_pixels, weight_in, weight_mid, weight_out, bias_hidden):
    region_ids = jnp.arange(REGIONS, dtype=jnp.int32)

    def run_forward(region):
        return forward(weight_in[region], weight_mid[region], weight_out[region], bias_hidden[region], grid_coords[:, region], segment_bounds[:, region], step_length[region], sample_depth[region])
    segments = lax.map(lambda region: run_forward(region)[0], region_ids)
    segment_grads = join_segments(jnp.transpose(segments, (1, 0, 2)), depth_rank.T, target_pixels, 1.0 / math.sqrt(TOTAL_RAYS))

    def run_backward(region):
        segment, cache = run_forward(region)
        return backward(weight_in[region], weight_mid[region], weight_out[region], step_length[region], sample_depth[region], cache, segment_grads[:, region])
    grad_in, grad_mid, grad_out, grad_bias = lax.map(run_backward, region_ids)
    return (grad_in, grad_mid, grad_out, grad_bias)
```

```python
import functools
import math

import jax
import jax.numpy as jnp
from jax import lax
from jax.experimental import pallas as pl
from jax.experimental.pallas import tpu as pltpu
from jax.sharding import PartitionSpec as P

GRID = 4096
LANES = 128
DEPTH_WEIGHT = 0.1
ENC_ROWS = 64

PI_HI = 3.140625
PI_MID = 9.67502593994140625e-4
PI_LO = 1.509957990978376432e-7

SIN_COEFS = (3.1415925798055784, -5.167706866167917, 2.5500311935189344, -0.5980441939097795, 0.07721838615261653)
COS_COEFS = (-4.934795324080539, 4.058447258699471, -1.332068065877436, 0.2200300516248938)

NT = (((1,), (1,)), ((), ()))


def dot(a, b):
    return jnp.dot(a, b, preferred_element_type=jnp.float32)


def dot_nt(a, b):
    return lax.dot_general(a, b, NT, preferred_element_type=jnp.float32)


def sigmoid(x):
    return 1.0 / (1.0 + jnp.exp(-x))


def softplus(x):
    z = jnp.exp(-jnp.abs(x))
    y = z / (2.0 + z)
    q = y * y
    series = 1.0 / 15.0
    for k in (13, 11, 9, 7, 5, 3, 1):
        series = series * q + 1.0 / k
    return jnp.maximum(x, 0.0) + 2.0 * y * series


def one_less_exp(x):
    small = 1.0 / 5040.0
    for k in (720, 120, 24, 6, 2, 1):
        small = 1.0 / k - x * small
    return jnp.where(x < 0.25, x * small, 1.0 - jnp.exp(-x))


def shift_down(rows):
    total = rows[0:1]
    out = [jnp.zeros_like(total), total]
    for s in range(1, rows.shape[0] - 1):
        total = total + rows[s : s + 1]
        out.append(total)
    return jnp.concatenate(out, axis=0)


def ray_terms(raw, step, first, last):
    slot = lax.broadcasted_iota(jnp.int32, step.shape, 0)
    live = ((slot >= first) & (slot < last)).astype(jnp.float32)
    density = softplus(raw[0])
    colour = [sigmoid(raw[c]) for c in (1, 2, 3)]
    optical = density * step * live
    before = shift_down(optical)
    blend = jnp.exp(-before) * one_less_exp(optical)
    return live, colour, optical, before, blend


def row_sum(x):
    return jnp.sum(x, axis=0, keepdims=True)


def forward_kernel(
    coords_ref, bounds_ref, step_ref, depth_ref, w_in_ref, w_mid_ref, w_out_ref, bias_ref,
    seg_ref, enc_ref, h1_ref, h2_ref, s1_ref, s2_ref, raw_ref,
    w1_ref, w2_ref, b2_ref, wide_ref, scale_ref, pos_ref,
):
    slots, rays = step_ref.shape[1], step_ref.shape[2]
    freqs = w_in_ref.shape[1] // 6

    @pl.when(pl.program_id(0) == 0)
    def _():
        wide_ref[...] = jnp.zeros_like(wide_ref)
        w_in = w_in_ref[0].astype(jnp.float32) * 0.5
        for part in range(2):
            for l in range(freqs):
                to = part * 32 + (l % 2) * 16 + (l // 2) * 3
                at = part * 3 * freqs + l * 3
                wide_ref[to : to + 3, :] = w_in[at : at + 3, :]
        half_bias = bias_ref[0] * 0.5
        upper = half_bias[0:1].astype(jnp.bfloat16).astype(jnp.float32)
        wide_ref[47:48, :] = upper
        wide_ref[63:64, :] = half_bias[0:1] - upper
        w1_ref[...] = wide_ref[...].T.astype(jnp.bfloat16)
        w2_ref[...] = (w_mid_ref[0].astype(jnp.float32) * 0.5).T.astype(jnp.bfloat16)
        b2_ref[...] = jnp.broadcast_to(half_bias[1:2], (LANES, half_bias.shape[1])).T
        row = lax.broadcasted_iota(jnp.int32, scale_ref.shape, 0)
        scale = jnp.zeros(scale_ref.shape, jnp.float32)
        for l in range(0, freqs, 2):
            scale = jnp.where(row // 3 == l // 2, 2.0 ** (l - 1), scale)
        scale_ref[...] = scale

    for c in range(3):
        p = (coords_ref[c, 0].astype(jnp.float32) + 0.5) * (1.0 / GRID)
        angle = p * math.pi
        error = ((angle - p * PI_HI) - p * PI_MID) - p * PI_LO
        pos_ref[c] = p
        pos_ref[3 + c] = error * (1.0 / math.pi)

    coord = lax.broadcasted_iota(jnp.int32, (16, rays), 0) % 3
    scale = scale_ref[...]
    b2 = jnp.concatenate([b2_ref[...]] * (rays // LANES), axis=1)
    for s in range(slots):
        rows = [jnp.broadcast_to(pos_ref[i, s : s + 1, :], (16, rays)) for i in range(6)]
        p = jnp.where(coord == 0, rows[0], jnp.where(coord == 1, rows[1], rows[2]))
        e = jnp.where(coord == 0, rows[3], jnp.where(coord == 1, rows[4], rows[5]))
        turns = p * scale
        r = (turns - jnp.round(turns)) + e * scale
        q = r * r
        sine = SIN_COEFS[4]
        for coef in SIN_COEFS[3::-1]:
            sine = sine * q + coef
        sine = sine * r
        cosine = COS_COEFS[3]
        for coef in COS_COEFS[2::-1]:
            cosine = cosine * q + coef
        cosine = cosine * q + 1.0
        twice = sine + sine
        sin_even = twice * cosine
        cos_even = 1.0 - twice * sine
        twice = sin_even + sin_even
        sin_odd = twice * cos_even
        cos_odd = 1.0 - twice * sin_even
        enc = jnp.concatenate([sin_even, sin_odd, cos_even, cos_odd], axis=0).astype(jnp.bfloat16)
        enc_ref[0, s] = enc

        def silu(half):
            w = jnp.tanh(half) + 1.0
            hidden = half * w
            return hidden.astype(jnp.bfloat16), (hidden * (2.0 - w) + w).astype(jnp.bfloat16)

        h1, s1 = silu(dot(w1_ref[...], enc))
        h1_ref[0, s] = h1
        s1_ref[0, s] = s1
        h2, s2 = silu(dot(w2_ref[...], h1) + b2)
        h2_ref[0, s] = h2
        s2_ref[0, s] = s2
        raw = dot(w_out_ref[0], h2)
        for c in range(4):
            raw_ref[0, c, s : s + 1, :] = raw[c : c + 1]

    raw = [raw_ref[0, c] for c in range(4)]
    step = step_ref[0]
    live, colour, optical, before, blend = ray_terms(raw, step, bounds_ref[0], bounds_ref[1])
    sums = [row_sum(blend * colour[c]) for c in range(3)]
    sums.append(row_sum(blend * depth_ref[0]))
    sums.append(-row_sum(optical))
    for j in range(rays // LANES):
        for i in range(5):
            seg_ref[j, i : i + 1, :] = sums[i][:, j * LANES : (j + 1) * LANES]


def join_kernel(region_ref, seg_ref, rank_ref, target_ref, out_ref, *, loss_scale):
    regions = seg_ref.shape[0]
    rank = rank_ref[...].astype(jnp.float32).T
    seg = [seg_ref[:, i, :] for i in range(5)]
    passing = jnp.zeros_like(rank)
    for r in range(regions):
        passing = passing + jnp.where(rank[r : r + 1] < rank, seg[4][r : r + 1], 0.0)
    light = jnp.exp(passing)
    grads = []
    weighted = jnp.zeros_like(light)
    for i in range(4):
        gain = 2.0 * loss_scale * (DEPTH_WEIGHT if i == 3 else 1.0)
        grad = gain * (row_sum(light * seg[i]) - target_ref[i : i + 1])
        grads.append(grad)
        weighted = weighted + grad * seg[i]
    terms = light * weighted
    later = jnp.zeros_like(terms)
    for r in range(regions):
        later = later + jnp.where(rank[r : r + 1] > rank, terms[r : r + 1], 0.0)
    for i in range(4):
        out_ref[:, i, :] = light * grads[i]
    out_ref[:, 4, :] = later


def backward_kernel(
    grad_ref, bounds_ref, step_ref, depth_ref, w_mid_ref, w_out_ref,
    enc_ref, h1_ref, h2_ref, s1_ref, s2_ref, raw_ref,
    out_ref,
    wm_ref, wo_ref, mid_ref, in_ref, outer_ref, bias_ref, gr_ref,
):
    slots, rays = step_ref.shape[1], step_ref.shape[2]

    @pl.when(pl.program_id(0) == 0)
    def _():
        wm_ref[...] = (w_mid_ref[0].astype(jnp.float32) * 0.5).astype(jnp.bfloat16)
        w_out = w_out_ref[0].astype(jnp.float32) * 0.5
        w_out = jnp.concatenate([w_out, jnp.zeros_like(w_out)], axis=0)
        wo_ref[...] = w_out.T.astype(jnp.bfloat16)
        mid_ref[...] = jnp.zeros_like(mid_ref)
        in_ref[...] = jnp.zeros_like(in_ref)
        outer_ref[...] = jnp.zeros_like(outer_ref)
        bias_ref[...] = jnp.zeros_like(bias_ref)
        gr_ref[...] = jnp.zeros_like(gr_ref)

    raw = [raw_ref[0, c] for c in range(4)]
    step = step_ref[0]
    live, colour, optical, before, blend = ray_terms(raw, step, bounds_ref[0], bounds_ref[1])
    grad = [
        jnp.concatenate([grad_ref[j, i : i + 1, :] for j in range(rays // LANES)], axis=1)
        for i in range(5)
    ]
    usage = grad[3] * depth_ref[0]
    for c in range(3):
        usage = usage + grad[c] * colour[c]
    weighted = usage * blend
    later = row_sum(weighted) - (shift_down(weighted) + weighted)
    grad_optical = usage * jnp.exp(-(before + optical)) - later - grad[4]
    grad_raw = [grad_optical * step * live * sigmoid(raw[0])]
    for c in range(3):
        grad_raw.append(grad[c] * blend * colour[c] * (1.0 - colour[c]))
    for s in range(slots):
        for c in range(4):
            gr_ref[s, c : c + 1, :] = grad_raw[c][s : s + 1]

    for s in range(slots):
        gr = gr_ref[s].astype(jnp.bfloat16)
        grad_two = dot(wo_ref[...], gr) * s2_ref[0, s].astype(jnp.float32)
        partial = bias_ref[...]
        for j in range(rays // LANES):
            partial = partial + grad_two[:, j * LANES : (j + 1) * LANES]
        bias_ref[...] = partial
        d2 = grad_two.astype(jnp.bfloat16)
        grad_one = dot(wm_ref[...], d2) * s1_ref[0, s].astype(jnp.float32)
        d1 = grad_one.astype(jnp.bfloat16)
        mid_ref[...] += dot_nt(d2, h1_ref[0, s])
        in_ref[...] += dot_nt(enc_ref[0, s], d1)
        outer_ref[...] += dot_nt(gr, h2_ref[0, s])

    @pl.when(pl.program_id(0) == pl.num_programs(0) - 1)
    def _():
        hid = mid_ref.shape[0]
        bias = jnp.sum(bias_ref[...], axis=1, keepdims=True)
        rest = jnp.concatenate([in_ref[...], outer_ref[...]], axis=0)
        rest = jnp.concatenate([rest, jnp.zeros((LANES - rest.shape[0], hid), jnp.float32)], axis=0).T
        lane = lax.broadcasted_iota(jnp.int32, rest.shape, 1)
        rest = jnp.where(lane == LANES - 1, bias, rest)
        parts, width = out_ref.shape[0], out_ref.shape[1]
        for k in range(parts):
            out_ref[k, :, :hid] = mid_ref[k * width : (k + 1) * width, :]
            out_ref[k, :, hid:] = rest[k * width : (k + 1) * width, :]


def finish_kernel(parts_ref, in_ref, mid_ref, out_ref, bias_ref):
    total = parts_ref[0]
    for k in range(1, parts_ref.shape[0]):
        total = total + parts_ref[k]
    hid = mid_ref.shape[1]
    freqs = in_ref.shape[1] // 6
    mid_ref[0] = total[:, :hid].T
    rest = total[:, hid:].T
    for part in range(2):
        for l in range(freqs):
            to = part * 32 + (l % 2) * 16 + (l // 2) * 3
            at = part * 3 * freqs + l * 3
            in_ref[0, at : at + 3, :] = rest[to : to + 3, :]
    out_ref[0] = rest[ENC_ROWS : ENC_ROWS + 4, :]
    bias_ref[0, 0:1, :] = rest[47:48, :]
    bias_ref[0, 1:2, :] = rest[LANES - 1 : LANES, :]


def whole(shape):
    return pl.BlockSpec(shape, lambda *_: (0,) * len(shape))


def on_device(
    grid_coords, segment_bounds, depth_rank, step_length, sample_depth,
    target_pixels, weight_in, weight_mid, weight_out, bias_hidden,
):
    f32, bf16 = jnp.float32, jnp.bfloat16
    _, slots, ray_count = step_length.shape
    regions = depth_rank.shape[1]
    enc, hid = weight_in.shape[1:]
    ways = lax.axis_size("rays")
    loss_scale = 1.0 / math.sqrt(ray_count * ways)
    rays = 512
    tiles = ray_count // rays
    chunk = rays // LANES
    arbitrary = pltpu.CompilerParams(dimension_semantics=("arbitrary",))

    ray_specs = [
        pl.BlockSpec((2, 1, rays), lambda t: (0, 0, t)),
        pl.BlockSpec((1, slots, rays), lambda t: (0, 0, t)),
        pl.BlockSpec((1, slots, rays), lambda t: (0, 0, t)),
    ]
    seg_spec = pl.BlockSpec((chunk, 8, LANES), lambda t: (t, 0, 0))
    save_specs = [
        pl.BlockSpec((1, slots, n, rays), lambda t: (t, 0, 0, 0))
        for n in (ENC_ROWS, hid, hid, hid, hid)
    ] + [pl.BlockSpec((1, 4, slots, rays), lambda t: (t, 0, 0, 0))]
    save_shapes = [
        jax.ShapeDtypeStruct((tiles, slots, n, rays), bf16) for n in (ENC_ROWS, hid, hid, hid, hid)
    ] + [jax.ShapeDtypeStruct((tiles, 4, slots, rays), f32)]

    outs = pl.pallas_call(
        forward_kernel,
        grid=(tiles,),
        in_specs=[pl.BlockSpec((3, 1, slots, rays), lambda t: (0, 0, 0, t))]
        + ray_specs
        + [whole(weight_in.shape), whole(weight_mid.shape), whole(weight_out.shape), whole(bias_hidden.shape)],
        out_specs=[seg_spec] + save_specs,
        out_shape=[jax.ShapeDtypeStruct((ray_count // LANES, 8, LANES), f32)] + save_shapes,
        scratch_shapes=[
            pltpu.VMEM((hid, ENC_ROWS), bf16),
            pltpu.VMEM((hid, hid), bf16),
            pltpu.VMEM((hid, LANES), f32),
            pltpu.VMEM((ENC_ROWS, hid), f32),
            pltpu.VMEM((16, rays), f32),
            pltpu.VMEM((6, slots, rays), f32),
        ],
        compiler_params=arbitrary,
        name="forward",
    )(grid_coords, segment_bounds, step_length, sample_depth, weight_in, weight_mid, weight_out, bias_hidden)
    segment, saved = outs[0], outs[1:]

    segments = lax.all_to_all(segment, "region", 0, 0, tiled=True)
    own = ray_count // regions
    position = lax.axis_index("region").astype(jnp.int32).reshape(1)
    joined = pl.pallas_call(
        functools.partial(join_kernel, loss_scale=loss_scale),
        grid_spec=pltpu.PrefetchScalarGridSpec(
            num_scalar_prefetch=1,
            grid=(1,),
            in_specs=[
                pl.BlockSpec((regions, 8, own), lambda t, at: (0, 0, 0)),
                pl.BlockSpec((own, regions), lambda t, at: (at[0], 0)),
                pl.BlockSpec((4, own), lambda t, at: (0, at[0])),
            ],
            out_specs=pl.BlockSpec((regions, 8, own), lambda t, at: (0, 0, 0)),
        ),
        out_shape=jax.ShapeDtypeStruct((regions, 8, own), f32),
        compiler_params=arbitrary,
        name="join",
    )(position, segments, depth_rank, target_pixels)
    segment_grad = lax.all_to_all(joined, "region", 0, 0, tiled=True)

    width = hid // ways
    grads = pl.pallas_call(
        backward_kernel,
        grid=(tiles,),
        in_specs=[seg_spec] + ray_specs + [whole(weight_mid.shape), whole(weight_out.shape)] + save_specs,
        out_specs=whole((ways, width, hid + LANES)),
        out_shape=jax.ShapeDtypeStruct((ways, width, hid + LANES), f32),
        scratch_shapes=[
            pltpu.VMEM((hid, hid), bf16),
            pltpu.VMEM((hid, 8), bf16),
            pltpu.VMEM((hid, hid), f32),
            pltpu.VMEM((ENC_ROWS, hid), f32),
            pltpu.VMEM((8, hid), f32),
            pltpu.VMEM((hid, LANES), f32),
            pltpu.VMEM((slots, 8, rays), f32),
        ],
        compiler_params=arbitrary,
        name="backward",
    )(segment_grad, segment_bounds, step_length, sample_depth, weight_mid, weight_out, *saved)

    parts = lax.all_to_all(grads, "rays", 0, 0, tiled=True)
    return tuple(
        pl.pallas_call(
            finish_kernel,
            out_shape=[
                jax.ShapeDtypeStruct((1, n, width), f32) for n in (enc, hid, 4, 2)
            ],
            name="finish",
        )(parts)
    )


def solution(mesh):
    placed = (
        P(None, "region", None, "rays"),
        P(None, "region", "rays"),
        P("rays", None),
        P("region", None, "rays"),
        P("region", None, "rays"),
        P(None, "rays"),
        P("region", None, None),
        P("region", None, None),
        P("region", None, None),
        P("region", None, None),
    )
    return jax.shard_map(
        on_device,
        mesh=mesh,
        in_specs=placed,
        out_specs=(P("region", None, "rays"),) * 4,
        check_vma=False,
    )
```

```python
import functools
import math

import jax
import jax.numpy as jnp
from jax import lax
from jax.experimental import pallas as pl
from jax.experimental.pallas import tpu as pltpu
from jax.sharding import PartitionSpec as P

GRID = 4096
LANES = 128
DEPTH_WEIGHT = 0.1
ENC_ROWS = 64

PI_HI = 3.140625
PI_MID = 9.67502593994140625e-4
PI_LO = 1.509957990978376432e-7

SIN_COEFS = (3.1415925798055784, -5.167706866167917, 2.5500311935189344, -0.5980441939097795, 0.07721838615261653)
COS_COEFS = (-4.934795324080539, 4.058447258699471, -1.332068065877436, 0.2200300516248938)

NT = (((1,), (1,)), ((), ()))


def dot(a, b):
    return jnp.dot(a, b, preferred_element_type=jnp.float32)


def dot_nt(a, b):
    return lax.dot_general(a, b, NT, preferred_element_type=jnp.float32)


def sigmoid(x):
    return 1.0 / (1.0 + jnp.exp(-x))


def softplus(x):
    z = jnp.exp(-jnp.abs(x))
    y = z / (2.0 + z)
    q = y * y
    series = 1.0 / 15.0
    for k in (13, 11, 9, 7, 5, 3, 1):
        series = series * q + 1.0 / k
    return jnp.maximum(x, 0.0) + 2.0 * y * series


def one_less_exp(x):
    small = 1.0 / 5040.0
    for k in (720, 120, 24, 6, 2, 1):
        small = 1.0 / k - x * small
    return jnp.where(x < 0.25, x * small, 1.0 - jnp.exp(-x))


def shift_down(rows):
    total = rows[0:1]
    out = [jnp.zeros_like(total), total]
    for s in range(1, rows.shape[0] - 1):
        total = total + rows[s : s + 1]
        out.append(total)
    return jnp.concatenate(out, axis=0)


def ray_terms(raw, step, first, last):
    slot = lax.broadcasted_iota(jnp.int32, step.shape, 0)
    live = ((slot >= first) & (slot < last)).astype(jnp.float32)
    density = softplus(raw[0])
    colour = [sigmoid(raw[c]) for c in (1, 2, 3)]
    optical = density * step * live
    before = shift_down(optical)
    blend = jnp.exp(-before) * one_less_exp(optical)
    return live, colour, optical, before, blend


def row_sum(x):
    return jnp.sum(x, axis=0, keepdims=True)


def put(ref, value):
    for j in range(ref.shape[1]):
        ref[0, j] = value[:, j * LANES : (j + 1) * LANES]


def take(ref, part=0, parts=1):
    tiles = ref.shape[1] // parts
    return jnp.concatenate([ref[0, j] for j in range(part * tiles, (part + 1) * tiles)], axis=1)


def silu(half):
    w = jnp.tanh(half) + 1.0
    hidden = half * w
    return hidden, hidden * (2.0 - w) + w


def forward_kernel(
    coords_ref, bounds_ref, step_ref, depth_ref, w_in_ref, w_mid_ref, w_out_ref, bias_ref,
    seg_ref, enc_ref, half1_ref, half2_ref, raw_ref,
    w1_ref, w2_ref, b2_ref, wide_ref, scale_ref, pos_ref,
):
    slots, rays = step_ref.shape[1], step_ref.shape[2]
    freqs = w_in_ref.shape[1] // 6

    @pl.when(pl.program_id(0) == 0)
    def _():
        wide_ref[...] = jnp.zeros_like(wide_ref)
        w_in = w_in_ref[0].astype(jnp.float32) * 0.5
        for part in range(2):
            for l in range(freqs):
                to = part * 32 + (l % 2) * 16 + (l // 2) * 3
                at = part * 3 * freqs + l * 3
                wide_ref[to : to + 3, :] = w_in[at : at + 3, :]
        half_bias = bias_ref[0] * 0.5
        upper = half_bias[0:1].astype(jnp.bfloat16).astype(jnp.float32)
        wide_ref[47:48, :] = upper
        wide_ref[63:64, :] = half_bias[0:1] - upper
        w1_ref[...] = wide_ref[...].T.astype(jnp.bfloat16)
        w2_ref[...] = (w_mid_ref[0].astype(jnp.float32) * 0.5).T.astype(jnp.bfloat16)
        b2_ref[...] = jnp.broadcast_to(half_bias[1:2], (LANES, half_bias.shape[1])).T
        row = lax.broadcasted_iota(jnp.int32, scale_ref.shape, 0)
        scale = jnp.zeros(scale_ref.shape, jnp.float32)
        for l in range(0, freqs, 2):
            scale = jnp.where(row // 3 == l // 2, 2.0 ** (l - 1), scale)
        scale_ref[...] = scale

    for c in range(3):
        p = (coords_ref[c, 0].astype(jnp.float32) + 0.5) * (1.0 / GRID)
        angle = p * math.pi
        error = ((angle - p * PI_HI) - p * PI_MID) - p * PI_LO
        pos_ref[c] = p
        pos_ref[3 + c] = error * (1.0 / math.pi)

    count = slots * rays
    coord = lax.broadcasted_iota(jnp.int32, (16, count), 0) % 3
    scale = scale_ref[...]
    rows = [
        jnp.broadcast_to(
            jnp.concatenate([pos_ref[i, s : s + 1, :] for s in range(slots)], axis=1), (16, count)
        )
        for i in range(6)
    ]
    p = jnp.where(coord == 0, rows[0], jnp.where(coord == 1, rows[1], rows[2]))
    e = jnp.where(coord == 0, rows[3], jnp.where(coord == 1, rows[4], rows[5]))
    turns = p * scale
    r = (turns - jnp.round(turns)) + e * scale
    q = r * r
    sine = SIN_COEFS[4]
    for coef in SIN_COEFS[3::-1]:
        sine = sine * q + coef
    sine = sine * r
    cosine = COS_COEFS[3]
    for coef in COS_COEFS[2::-1]:
        cosine = cosine * q + coef
    cosine = cosine * q + 1.0
    twice = sine + sine
    sin_even = twice * cosine
    cos_even = 1.0 - twice * sine
    twice = sin_even + sin_even
    sin_odd = twice * cos_even
    cos_odd = 1.0 - twice * sin_even
    enc = jnp.concatenate([sin_even, sin_odd, cos_even, cos_odd], axis=0).astype(jnp.bfloat16)
    enc_ref[0] = enc
    half = dot(w1_ref[...], enc).astype(jnp.bfloat16)
    put(half1_ref, half)
    hidden, _ = silu(half)
    b2 = jnp.concatenate([b2_ref[...]] * (count // LANES), axis=1)
    half = (dot(w2_ref[...], hidden) + b2).astype(jnp.bfloat16)
    put(half2_ref, half)
    hidden, _ = silu(half)
    raw_all = dot(w_out_ref[0], hidden)
    for s in range(slots):
        for c in range(4):
            raw_ref[0, c, s : s + 1, :] = raw_all[c : c + 1, s * rays : (s + 1) * rays]

    raw = [raw_ref[0, c] for c in range(4)]
    step = step_ref[0]
    live, colour, optical, before, blend = ray_terms(raw, step, bounds_ref[0], bounds_ref[1])
    sums = [row_sum(blend * colour[c]) for c in range(3)]
    sums.append(row_sum(blend * depth_ref[0]))
    sums.append(-row_sum(optical))
    for j in range(rays // LANES):
        for i in range(5):
            seg_ref[j, i : i + 1, :] = sums[i][:, j * LANES : (j + 1) * LANES]


def join_kernel(region_ref, seg_ref, rank_ref, target_ref, out_ref, *, loss_scale):
    regions = seg_ref.shape[0]
    rank = rank_ref[...]
    seg = [seg_ref[:, i, :] for i in range(5)]
    passing = jnp.zeros_like(rank)
    for r in range(regions):
        passing = passing + jnp.where(rank[r : r + 1] < rank, seg[4][r : r + 1], 0.0)
    light = jnp.exp(passing)
    grads = []
    weighted = jnp.zeros_like(light)
    for i in range(4):
        gain = 2.0 * loss_scale * (DEPTH_WEIGHT if i == 3 else 1.0)
        grad = gain * (row_sum(light * seg[i]) - target_ref[i : i + 1])
        grads.append(grad)
        weighted = weighted + grad * seg[i]
    terms = light * weighted
    later = jnp.zeros_like(terms)
    for r in range(regions):
        later = later + jnp.where(rank[r : r + 1] > rank, terms[r : r + 1], 0.0)
    for i in range(4):
        out_ref[:, i, :] = light * grads[i]
    out_ref[:, 4, :] = later


def backward_kernel(
    grad_ref, bounds_ref, step_ref, depth_ref, w_mid_ref, w_out_ref,
    enc_ref, half1_ref, half2_ref, raw_ref,
    out_ref,
    wm_ref, wo_ref, mid_ref, in_ref, outer_ref, gr_ref,
):
    slots, rays = step_ref.shape[1], step_ref.shape[2]

    @pl.when(pl.program_id(0) == 0)
    def _():
        wm_ref[...] = (w_mid_ref[0].astype(jnp.float32) * 0.5).astype(jnp.bfloat16)
        w_out = w_out_ref[0].astype(jnp.float32) * 0.5
        w_out = jnp.concatenate([w_out, jnp.zeros_like(w_out)], axis=0)
        wo_ref[...] = w_out.T.astype(jnp.bfloat16)
        mid_ref[...] = jnp.zeros_like(mid_ref)
        in_ref[...] = jnp.zeros_like(in_ref)
        outer_ref[...] = jnp.zeros_like(outer_ref)
        gr_ref[...] = jnp.zeros_like(gr_ref)

    raw = [raw_ref[0, c] for c in range(4)]
    step = step_ref[0]
    live, colour, optical, before, blend = ray_terms(raw, step, bounds_ref[0], bounds_ref[1])
    grad = [
        jnp.concatenate([grad_ref[j, i : i + 1, :] for j in range(rays // LANES)], axis=1)
        for i in range(5)
    ]
    usage = grad[3] * depth_ref[0]
    for c in range(3):
        usage = usage + grad[c] * colour[c]
    weighted = usage * blend
    later = row_sum(weighted) - (shift_down(weighted) + weighted)
    grad_optical = usage * jnp.exp(-(before + optical)) - later - grad[4]
    grad_raw = [grad_optical * step * live * sigmoid(raw[0])]
    for c in range(3):
        grad_raw.append(grad[c] * blend * colour[c] * (1.0 - colour[c]))
    count = slots * rays
    for s in range(slots):
        for c in range(4):
            gr_ref[c : c + 1, s * rays : (s + 1) * rays] = grad_raw[c][s : s + 1]

    gr = gr_ref[...].astype(jnp.bfloat16)
    grad_two = dot(wo_ref[...], gr).astype(jnp.bfloat16)
    hidden_two, slope = silu(take(half2_ref))
    d2 = grad_two * slope
    grad_one = dot(wm_ref[...], d2).astype(jnp.bfloat16)
    hidden, slope = silu(take(half1_ref))
    d1 = grad_one * slope
    ones = jnp.ones((16, count), jnp.bfloat16)
    mid_ref[...] += dot_nt(jnp.concatenate([hidden, ones], axis=0), d2)
    outer_ref[...] += dot_nt(gr, hidden_two)
    in_ref[...] += dot_nt(enc_ref[0], d1)

    @pl.when(pl.program_id(0) == pl.num_programs(0) - 1)
    def _():
        hid = mid_ref.shape[1]
        blank = jnp.zeros((LANES - ENC_ROWS - 24, hid), jnp.float32)
        rest = jnp.concatenate([in_ref[...], mid_ref[hid:, :], outer_ref[...], blank], axis=0).T
        mid = mid_ref[:hid, :].T
        parts, width = out_ref.shape[0], out_ref.shape[1]
        for k in range(parts):
            out_ref[k, :, :hid] = mid[k * width : (k + 1) * width, :]
            out_ref[k, :, hid:] = rest[k * width : (k + 1) * width, :]


def finish_kernel(parts_ref, in_ref, mid_ref, out_ref, bias_ref):
    total = parts_ref[0]
    for k in range(1, parts_ref.shape[0]):
        total = total + parts_ref[k]
    hid = mid_ref.shape[2]
    freqs = in_ref.shape[2] // 6
    mid_ref[0] = total[:, :hid]
    rest = total[:, hid:].T
    rows = []
    for part in range(2):
        for l in range(freqs):
            at = part * 32 + (l % 2) * 16 + (l // 2) * 3
            rows.append(rest[at : at + 3, :])
    in_ref[0] = jnp.concatenate(rows, axis=0).T
    out_ref[0] = rest[ENC_ROWS + 16 : ENC_ROWS + 20, :]
    bias_ref[0, 0:1, :] = rest[47:48, :]
    bias_ref[0, 1:2, :] = rest[ENC_ROWS : ENC_ROWS + 1, :]


def whole(shape):
    return pl.BlockSpec(shape, lambda *_: (0,) * len(shape))


def on_device(
    grid_coords, segment_bounds, depth_rank, step_length, sample_depth,
    target_pixels, weight_in, weight_mid, weight_out, bias_hidden,
):
    f32, bf16 = jnp.float32, jnp.bfloat16
    _, slots, ray_count = step_length.shape
    regions = depth_rank.shape[1]
    enc, hid = weight_in.shape[1:]
    ways = lax.axis_size("rays")
    loss_scale = 1.0 / math.sqrt(ray_count * ways)
    rays = 512
    tiles = ray_count // rays
    chunk = rays // LANES
    arbitrary = pltpu.CompilerParams(dimension_semantics=("arbitrary",))

    lp = pltpu.CompilerParams(dimension_semantics=("arbitrary",))

    ray_specs = [
        pl.BlockSpec((2, 1, rays), lambda t: (0, 0, t)),
        pl.BlockSpec((1, slots, rays), lambda t: (0, 0, t)),
        pl.BlockSpec((1, slots, rays), lambda t: (0, 0, t)),
    ]
    seg_spec = pl.BlockSpec((chunk, 8, LANES), lambda t: (t, 0, 0))
    save_specs = (
        [pl.BlockSpec((1, ENC_ROWS, slots * rays), lambda t: (t, 0, 0))]
        + [pl.BlockSpec((1, slots * chunk, hid, LANES), lambda t: (t, 0, 0, 0))] * 2
        + [pl.BlockSpec((1, 4, slots, rays), lambda t: (t, 0, 0, 0))]
    )
    save_shapes = (
        [jax.ShapeDtypeStruct((tiles, ENC_ROWS, slots * rays), bf16)]
        + [jax.ShapeDtypeStruct((tiles, slots * chunk, hid, LANES), bf16)] * 2
        + [jax.ShapeDtypeStruct((tiles, 4, slots, rays), f32)]
    )

    outs = pl.pallas_call(
        forward_kernel,
        grid=(tiles,),
        in_specs=[pl.BlockSpec((3, 1, slots, rays), lambda t: (0, 0, 0, t))]
        + ray_specs
        + [whole(weight_in.shape), whole(weight_mid.shape), whole(weight_out.shape), whole(bias_hidden.shape)],
        out_specs=[seg_spec] + save_specs,
        out_shape=[jax.ShapeDtypeStruct((ray_count // LANES, 8, LANES), f32)] + save_shapes,
        scratch_shapes=[
            pltpu.VMEM((hid, ENC_ROWS), bf16),
            pltpu.VMEM((hid, hid), bf16),
            pltpu.VMEM((hid, LANES), f32),
            pltpu.VMEM((ENC_ROWS, hid), f32),
            pltpu.VMEM((16, slots * rays), f32),
            pltpu.VMEM((6, slots, rays), f32),
        ],
        compiler_params=arbitrary,
        name="forward",
    )(grid_coords, segment_bounds, step_length, sample_depth, weight_in, weight_mid, weight_out, bias_hidden)
    segment, saved = outs[0], outs[1:]

    segments = lax.all_to_all(segment, "region", 0, 0, tiled=True)
    own = ray_count // regions
    position = lax.axis_index("region").astype(jnp.int32).reshape(1)
    joined = pl.pallas_call(
        functools.partial(join_kernel, loss_scale=loss_scale),
        grid_spec=pltpu.PrefetchScalarGridSpec(
            num_scalar_prefetch=1,
            grid=(1,),
            in_specs=[
                pl.BlockSpec((regions, 8, own), lambda t, at: (0, 0, 0)),
                pl.BlockSpec((regions, own), lambda t, at: (0, at[0])),
                pl.BlockSpec((4, own), lambda t, at: (0, at[0])),
            ],
            out_specs=pl.BlockSpec((regions, 8, own), lambda t, at: (0, 0, 0)),
        ),
        out_shape=jax.ShapeDtypeStruct((regions, 8, own), f32),
        compiler_params=arbitrary,
        name="join",
    )(position, segments, depth_rank.T, target_pixels)
    segment_grad = lax.all_to_all(joined, "region", 0, 0, tiled=True)

    width = hid // ways
    grads = pl.pallas_call(
        backward_kernel,
        grid=(tiles,),
        in_specs=[seg_spec] + ray_specs + [whole(weight_mid.shape), whole(weight_out.shape)] + save_specs,
        out_specs=whole((ways, width, hid + LANES)),
        out_shape=jax.ShapeDtypeStruct((ways, width, hid + LANES), f32),
        scratch_shapes=[
            pltpu.VMEM((hid, hid), bf16),
            pltpu.VMEM((hid, 8), bf16),
            pltpu.VMEM((hid + 16, hid), f32),
            pltpu.VMEM((ENC_ROWS, hid), f32),
            pltpu.VMEM((8, hid), f32),
            pltpu.VMEM((8, slots * rays), f32),
        ],
        compiler_params=lp,
        name="backward",
    )(segment_grad, segment_bounds, step_length, sample_depth, weight_mid, weight_out, *saved)

    parts = lax.all_to_all(grads, "rays", 0, 0, tiled=True)
    grad_in, grad_mid, grad_out, grad_bias = pl.pallas_call(
        finish_kernel,
        out_shape=[
            jax.ShapeDtypeStruct(shape, f32)
            for shape in ((1, width, enc), (1, width, hid), (1, 4, width), (1, 2, width))
        ],
        name="finish",
    )(parts)
    return jnp.swapaxes(grad_in, 1, 2), jnp.swapaxes(grad_mid, 1, 2), grad_out, grad_bias


def solution(mesh):
    placed = (
        P(None, "region", None, "rays"),
        P(None, "region", "rays"),
        P("rays", None),
        P("region", None, "rays"),
        P("region", None, "rays"),
        P(None, "rays"),
        P("region", None, None),
        P("region", None, None),
        P("region", None, None),
        P("region", None, None),
    )
    return jax.shard_map(
        on_device,
        mesh=mesh,
        in_specs=placed,
        out_specs=(P("region", None, "rays"),) * 4,
        check_vma=False,
    )
```

```python
import functools
import math

import jax
import jax.numpy as jnp
from jax import lax
from jax.experimental import pallas as pl
from jax.experimental.pallas import tpu as pltpu
from jax.sharding import PartitionSpec as P

GRID = 4096
LANES = 128
DEPTH_WEIGHT = 0.1
ENC_ROWS = 64

PI_HI = 3.140625
PI_MID = 9.67502593994140625e-4
PI_LO = 1.509957990978376432e-7

SIN_COEFS = (3.1415925798055784, -5.167706866167917, 2.5500311935189344, -0.5980441939097795, 0.07721838615261653)
COS_COEFS = (-4.934795324080539, 4.058447258699471, -1.332068065877436, 0.2200300516248938)

NT = (((1,), (1,)), ((), ()))


def dot(a, b):
    return jnp.dot(a, b, preferred_element_type=jnp.float32)


def dot_nt(a, b):
    return lax.dot_general(a, b, NT, preferred_element_type=jnp.float32)


def sigmoid(x):
    return 1.0 / (1.0 + jnp.exp(-x))


def softplus(x):
    z = jnp.exp(-jnp.abs(x))
    y = z / (2.0 + z)
    q = y * y
    series = 1.0 / 15.0
    for k in (13, 11, 9, 7, 5, 3, 1):
        series = series * q + 1.0 / k
    return jnp.maximum(x, 0.0) + 2.0 * y * series


def one_less_exp(x):
    small = 1.0 / 5040.0
    for k in (720, 120, 24, 6, 2, 1):
        small = 1.0 / k - x * small
    return jnp.where(x < 0.25, x * small, 1.0 - jnp.exp(-x))


def shift_down(rows):
    total = rows[0:1]
    out = [jnp.zeros_like(total), total]
    for s in range(1, rows.shape[0] - 1):
        total = total + rows[s : s + 1]
        out.append(total)
    return jnp.concatenate(out, axis=0)


def ray_terms(raw, step, first, last):
    slot = lax.broadcasted_iota(jnp.int32, step.shape, 0)
    live = ((slot >= first) & (slot < last)).astype(jnp.float32)
    density = softplus(raw[0])
    colour = [sigmoid(raw[c]) for c in (1, 2, 3)]
    optical = density * step * live
    before = shift_down(optical)
    blend = jnp.exp(-before) * one_less_exp(optical)
    return live, colour, optical, before, blend


def row_sum(x):
    return jnp.sum(x, axis=0, keepdims=True)


def put(ref, value):
    for j in range(ref.shape[1]):
        ref[0, j] = value[:, j * LANES : (j + 1) * LANES]


def take(ref, part=0, parts=1):
    tiles = ref.shape[1] // parts
    return jnp.concatenate([ref[0, j] for j in range(part * tiles, (part + 1) * tiles)], axis=1)


def silu(half):
    w = jnp.tanh(half) + 1.0
    hidden = half * w
    return hidden, hidden * (2.0 - w) + w


def forward_kernel(
    coords_ref, bounds_ref, step_ref, depth_ref, w_in_ref, w_mid_ref, w_out_ref, bias_ref,
    seg_ref, enc_ref, half1_ref, half2_ref, raw_ref,
    w1_ref, w2_ref, b2_ref, wide_ref, scale_ref, pos_ref,
):
    slots, rays = step_ref.shape[1], step_ref.shape[2]
    freqs = w_in_ref.shape[1] // 6

    @pl.when(pl.program_id(0) == 0)
    def _():
        wide_ref[...] = jnp.zeros_like(wide_ref)
        w_in = w_in_ref[0].astype(jnp.float32) * 0.5
        for part in range(2):
            for l in range(freqs):
                to = part * 32 + (l % 2) * 16 + (l // 2) * 3
                at = part * 3 * freqs + l * 3
                wide_ref[to : to + 3, :] = w_in[at : at + 3, :]
        half_bias = bias_ref[0] * 0.5
        upper = half_bias[0:1].astype(jnp.bfloat16).astype(jnp.float32)
        wide_ref[47:48, :] = upper
        wide_ref[63:64, :] = half_bias[0:1] - upper
        w1_ref[...] = wide_ref[...].T.astype(jnp.bfloat16)
        w2_ref[...] = (w_mid_ref[0].astype(jnp.float32) * 0.5).T.astype(jnp.bfloat16)
        b2_ref[...] = jnp.broadcast_to(half_bias[1:2], (LANES, half_bias.shape[1])).T
        row = lax.broadcasted_iota(jnp.int32, scale_ref.shape, 0)
        scale = jnp.zeros(scale_ref.shape, jnp.float32)
        for l in range(0, freqs, 2):
            scale = jnp.where(row // 3 == l // 2, 2.0 ** (l - 1), scale)
        scale_ref[...] = scale

    for c in range(3):
        p = (coords_ref[c, 0].astype(jnp.float32) + 0.5) * (1.0 / GRID)
        angle = p * math.pi
        error = ((angle - p * PI_HI) - p * PI_MID) - p * PI_LO
        pos_ref[c] = p
        pos_ref[3 + c] = error * (1.0 / math.pi)

    count = slots * rays
    coord = lax.broadcasted_iota(jnp.int32, (16, count), 0) % 3
    scale = scale_ref[...]
    rows = [
        jnp.broadcast_to(
            jnp.concatenate([pos_ref[i, s : s + 1, :] for s in range(slots)], axis=1), (16, count)
        )
        for i in range(6)
    ]
    p = jnp.where(coord == 0, rows[0], jnp.where(coord == 1, rows[1], rows[2]))
    e = jnp.where(coord == 0, rows[3], jnp.where(coord == 1, rows[4], rows[5]))
    turns = p * scale
    r = (turns - jnp.round(turns)) + e * scale
    q = r * r
    sine = SIN_COEFS[4]
    for coef in SIN_COEFS[3::-1]:
        sine = sine * q + coef
    sine = sine * r
    cosine = COS_COEFS[3]
    for coef in COS_COEFS[2::-1]:
        cosine = cosine * q + coef
    cosine = cosine * q + 1.0
    twice = sine + sine
    sin_even = twice * cosine
    cos_even = 1.0 - twice * sine
    twice = sin_even + sin_even
    sin_odd = twice * cos_even
    cos_odd = 1.0 - twice * sin_even
    enc = jnp.concatenate([sin_even, sin_odd, cos_even, cos_odd], axis=0).astype(jnp.bfloat16)
    enc_ref[0] = enc
    half = dot(w1_ref[...], enc).astype(jnp.bfloat16)
    put(half1_ref, half)
    hidden, _ = silu(half)
    b2 = jnp.concatenate([b2_ref[...]] * (count // LANES), axis=1)
    half = (dot(w2_ref[...], hidden) + b2).astype(jnp.bfloat16)
    put(half2_ref, half)
    hidden, _ = silu(half)
    raw_all = dot(w_out_ref[0], hidden)
    for s in range(slots):
        for c in range(4):
            raw_ref[0, c, s : s + 1, :] = raw_all[c : c + 1, s * rays : (s + 1) * rays]

    raw = [raw_ref[0, c] for c in range(4)]
    step = step_ref[0]
    live, colour, optical, before, blend = ray_terms(raw, step, bounds_ref[0], bounds_ref[1])
    sums = [row_sum(blend * colour[c]) for c in range(3)]
    sums.append(row_sum(blend * depth_ref[0]))
    sums.append(-row_sum(optical))
    for j in range(rays // LANES):
        for i in range(5):
            seg_ref[j, i : i + 1, :] = sums[i][:, j * LANES : (j + 1) * LANES]


def join_kernel(region_ref, seg_ref, rank_ref, target_ref, out_ref, *, loss_scale):
    regions = seg_ref.shape[0]
    rank = rank_ref[...]
    seg = [seg_ref[:, i, :] for i in range(5)]
    passing = jnp.zeros_like(rank)
    for r in range(regions):
        passing = passing + jnp.where(rank[r : r + 1] < rank, seg[4][r : r + 1], 0.0)
    light = jnp.exp(passing)
    grads = []
    weighted = jnp.zeros_like(light)
    for i in range(4):
        gain = 2.0 * loss_scale * (DEPTH_WEIGHT if i == 3 else 1.0)
        grad = gain * (row_sum(light * seg[i]) - target_ref[i : i + 1])
        grads.append(grad)
        weighted = weighted + grad * seg[i]
    terms = light * weighted
    later = jnp.zeros_like(terms)
    for r in range(regions):
        later = later + jnp.where(rank[r : r + 1] > rank, terms[r : r + 1], 0.0)
    for i in range(4):
        out_ref[:, i, :] = light * grads[i]
    out_ref[:, 4, :] = later


def backward_kernel(
    place_ref, grad_ref, bounds_ref, step_ref, depth_ref, w_mid_ref, w_out_ref,
    enc_ref, half1_ref, half2_ref, raw_ref,
    mine_ref, other_ref,
    wm_ref, wo_ref, mid_ref, in_ref, outer_ref, gr_ref, all_ref,
):
    slots, rays = step_ref.shape[1], step_ref.shape[2]

    @pl.when(pl.program_id(0) == 0)
    def _():
        wm_ref[...] = (w_mid_ref[0].astype(jnp.float32) * 0.5).astype(jnp.bfloat16)
        w_out = w_out_ref[0].astype(jnp.float32) * 0.5
        w_out = jnp.concatenate([w_out, jnp.zeros_like(w_out)], axis=0)
        wo_ref[...] = w_out.T.astype(jnp.bfloat16)
        mid_ref[...] = jnp.zeros_like(mid_ref)
        in_ref[...] = jnp.zeros_like(in_ref)
        outer_ref[...] = jnp.zeros_like(outer_ref)
        gr_ref[...] = jnp.zeros_like(gr_ref)

    raw = [raw_ref[0, c] for c in range(4)]
    step = step_ref[0]
    live, colour, optical, before, blend = ray_terms(raw, step, bounds_ref[0], bounds_ref[1])
    grad = [
        jnp.concatenate([grad_ref[j, i : i + 1, :] for j in range(rays // LANES)], axis=1)
        for i in range(5)
    ]
    usage = grad[3] * depth_ref[0]
    for c in range(3):
        usage = usage + grad[c] * colour[c]
    weighted = usage * blend
    later = row_sum(weighted) - (shift_down(weighted) + weighted)
    grad_optical = usage * jnp.exp(-(before + optical)) - later - grad[4]
    grad_raw = [grad_optical * step * live * sigmoid(raw[0])]
    for c in range(3):
        grad_raw.append(grad[c] * blend * colour[c] * (1.0 - colour[c]))
    count = slots * rays
    for s in range(slots):
        for c in range(4):
            gr_ref[c : c + 1, s * rays : (s + 1) * rays] = grad_raw[c][s : s + 1]

    gr = gr_ref[...].astype(jnp.bfloat16)
    grad_two = dot(wo_ref[...], gr).astype(jnp.bfloat16)
    hidden_two, slope_two = silu(take(half2_ref))
    d2 = grad_two * slope_two
    grad_one = dot(wm_ref[...], d2).astype(jnp.bfloat16)
    hidden, slope = silu(take(half1_ref))
    d1 = grad_one * slope
    in_ref[...] += dot_nt(enc_ref[0], d1)
    ones = jnp.ones((16, count), jnp.bfloat16)
    mid_ref[...] += dot_nt(jnp.concatenate([hidden, ones], axis=0), d2)
    outer_ref[...] += dot_nt(gr, hidden_two)

    @pl.when(pl.program_id(0) == pl.num_programs(0) - 1)
    def _():
        hid = mid_ref.shape[1]
        blank = jnp.zeros((LANES - ENC_ROWS - 24, hid), jnp.float32)
        rest = jnp.concatenate([in_ref[...], mid_ref[hid:, :], outer_ref[...], blank], axis=0)
        all_ref[:, hid:] = rest.T
        all_ref[:, :hid] = mid_ref[:hid, :].T
        chips, width = mine_ref.shape[:2]
        chip = place_ref[0] // 2
        core = place_ref[0] % 2
        for k in range(chips):
            pair = lax.rem(chip + k, chips) * 2
            mine_ref[k] = all_ref[pl.ds(pl.multiple_of((pair + core) * width, width), width), :]
            other_ref[k] = all_ref[pl.ds(pl.multiple_of((pair + 1 - core) * width, width), width), :]


def finish_kernel(own_ref, one_ref, two_ref, three_ref, in_ref, mid_ref, out_ref, bias_ref):
    total = (own_ref[...] + one_ref[...]) + (two_ref[...] + three_ref[...])
    hid = mid_ref.shape[2]
    freqs = in_ref.shape[2] // 6
    mid_ref[0] = total[:, :hid]
    rest = total[:, hid:].T
    rows = []
    for part in range(2):
        for l in range(freqs):
            at = part * 32 + (l % 2) * 16 + (l // 2) * 3
            rows.append(rest[at : at + 3, :])
    in_ref[0] = jnp.concatenate(rows, axis=0).T
    out_ref[0] = rest[ENC_ROWS + 16 : ENC_ROWS + 20, :]
    bias_ref[0, 0:1, :] = rest[47:48, :]
    bias_ref[0, 1:2, :] = rest[ENC_ROWS : ENC_ROWS + 1, :]


def whole(shape):
    return pl.BlockSpec(shape, lambda *_: (0,) * len(shape))


def on_device(
    grid_coords, segment_bounds, depth_rank, step_length, sample_depth,
    target_pixels, weight_in, weight_mid, weight_out, bias_hidden,
):
    f32, bf16 = jnp.float32, jnp.bfloat16
    _, slots, ray_count = step_length.shape
    regions = depth_rank.shape[1]
    enc, hid = weight_in.shape[1:]
    ways = lax.axis_size("rays")
    loss_scale = 1.0 / math.sqrt(ray_count * ways)
    rays = 512
    tiles = ray_count // rays
    chunk = rays // LANES
    arbitrary = pltpu.CompilerParams(dimension_semantics=("arbitrary",))

    small = pltpu.CompilerParams(vmem_limit_bytes=4 << 20)
    lp = pltpu.CompilerParams(dimension_semantics=("arbitrary",))

    ray_specs = [
        pl.BlockSpec((2, 1, rays), lambda t: (0, 0, t)),
        pl.BlockSpec((1, slots, rays), lambda t: (0, 0, t)),
        pl.BlockSpec((1, slots, rays), lambda t: (0, 0, t)),
    ]
    seg_spec = pl.BlockSpec((chunk, 8, LANES), lambda t: (t, 0, 0))
    save_specs = (
        [pl.BlockSpec((1, ENC_ROWS, slots * rays), lambda t: (t, 0, 0))]
        + [pl.BlockSpec((1, slots * chunk, hid, LANES), lambda t: (t, 0, 0, 0))] * 2
        + [pl.BlockSpec((1, 4, slots, rays), lambda t: (t, 0, 0, 0))]
    )
    save_shapes = (
        [jax.ShapeDtypeStruct((tiles, ENC_ROWS, slots * rays), bf16)]
        + [jax.ShapeDtypeStruct((tiles, slots * chunk, hid, LANES), bf16)] * 2
        + [jax.ShapeDtypeStruct((tiles, 4, slots, rays), f32)]
    )

    outs = pl.pallas_call(
        forward_kernel,
        grid=(tiles,),
        in_specs=[pl.BlockSpec((3, 1, slots, rays), lambda t: (0, 0, 0, t))]
        + ray_specs
        + [whole(weight_in.shape), whole(weight_mid.shape), whole(weight_out.shape), whole(bias_hidden.shape)],
        out_specs=[seg_spec] + save_specs,
        out_shape=[jax.ShapeDtypeStruct((ray_count // LANES, 8, LANES), f32)] + save_shapes,
        scratch_shapes=[
            pltpu.VMEM((hid, ENC_ROWS), bf16),
            pltpu.VMEM((hid, hid), bf16),
            pltpu.VMEM((hid, LANES), f32),
            pltpu.VMEM((ENC_ROWS, hid), f32),
            pltpu.VMEM((16, slots * rays), f32),
            pltpu.VMEM((6, slots, rays), f32),
        ],
        compiler_params=arbitrary,
        name="forward",
    )(grid_coords, segment_bounds, step_length, sample_depth, weight_in, weight_mid, weight_out, bias_hidden)
    segment, saved = outs[0], outs[1:]

    segments = lax.all_to_all(segment, "region", 0, 0, tiled=True)
    own = ray_count // regions
    position = lax.axis_index("region").astype(jnp.int32).reshape(1)
    joined = pl.pallas_call(
        functools.partial(join_kernel, loss_scale=loss_scale),
        grid_spec=pltpu.PrefetchScalarGridSpec(
            num_scalar_prefetch=1,
            grid=(1,),
            in_specs=[
                pl.BlockSpec((regions, 8, own), lambda t, at: (0, 0, 0)),
                pl.BlockSpec((regions, own), lambda t, at: (0, at[0])),
                pl.BlockSpec((4, own), lambda t, at: (0, at[0])),
            ],
            out_specs=pl.BlockSpec((regions, 8, own), lambda t, at: (0, 0, 0)),
        ),
        out_shape=jax.ShapeDtypeStruct((regions, 8, own), f32),
        compiler_params=arbitrary,
        name="join",
    )(position, segments, depth_rank.T, target_pixels)
    segment_grad = lax.all_to_all(joined, "region", 0, 0, tiled=True)

    width = hid // ways
    chips = ways // 2

    def at(spec):
        return pl.BlockSpec(spec.block_shape, lambda t, _: spec.index_map(t))

    place = lax.axis_index("rays").astype(jnp.int32).reshape(1)
    mine, other = pl.pallas_call(
        backward_kernel,
        grid_spec=pltpu.PrefetchScalarGridSpec(
            num_scalar_prefetch=1,
            grid=(tiles,),
            in_specs=[
                at(spec)
                for spec in [seg_spec] + ray_specs + [whole(weight_mid.shape), whole(weight_out.shape)] + save_specs
            ],
            out_specs=[whole((chips, width, hid + LANES))] * 2,
            scratch_shapes=[
                pltpu.VMEM((hid, hid), bf16),
                pltpu.VMEM((hid, 8), bf16),
                pltpu.VMEM((hid + 16, hid), f32),
                pltpu.VMEM((ENC_ROWS, hid), f32),
                pltpu.VMEM((8, hid), f32),
                pltpu.VMEM((8, slots * rays), f32),
                pltpu.VMEM((hid, hid + LANES), f32),
            ],
        ),
        out_shape=[jax.ShapeDtypeStruct((chips, width, hid + LANES), f32)] * 2,
        compiler_params=lp,
        name="backward",
    )(place, segment_grad, segment_bounds, step_length, sample_depth, weight_mid, weight_out, *saved)

    arrived = lax.ppermute(other, "rays", [(i, i ^ 1) for i in range(ways)])
    pairs = [mine[k] + arrived[k] for k in range(chips)]
    parts = [pairs[0]] + [
        lax.ppermute(pairs[k], "rays", [(i, (i + 2 * k) % ways) for i in range(ways)])
        for k in range(1, chips)
    ]
    grad_in, grad_mid, grad_out, grad_bias = pl.pallas_call(
        finish_kernel,
        out_shape=[
            jax.ShapeDtypeStruct(shape, f32)
            for shape in ((1, width, enc), (1, width, hid), (1, 4, width), (1, 2, width))
        ],
        compiler_params=small,
        name="finish",
    )(*parts)
    return jnp.swapaxes(grad_in, 1, 2), jnp.swapaxes(grad_mid, 1, 2), grad_out, grad_bias


def solution(mesh):
    placed = (
        P(None, "region", None, "rays"),
        P(None, "region", "rays"),
        P("rays", None),
        P("region", None, "rays"),
        P("region", None, "rays"),
        P(None, "rays"),
        P("region", None, None),
        P("region", None, None),
        P("region", None, None),
        P("region", None, None),
    )
    return jax.shard_map(
        on_device,
        mesh=mesh,
        in_specs=placed,
        out_specs=(P("region", None, "rays"),) * 4,
        check_vma=False,
    )
```

```python
import functools
import math

import jax
import jax.numpy as jnp
from jax import lax
from jax.experimental import pallas as pl
from jax.experimental.pallas import tpu as pltpu
from jax.sharding import PartitionSpec as P

GRID = 4096
LANES = 128
DEPTH_WEIGHT = 0.1
ENC_ROWS = 64

PI_HI = 3.140625
PI_MID = 9.67502593994140625e-4
PI_LO = 1.509957990978376432e-7

SIN_COEFS = (3.1415925798055784, -5.167706866167917, 2.5500311935189344, -0.5980441939097795, 0.07721838615261653)
COS_COEFS = (-4.934795324080539, 4.058447258699471, -1.332068065877436, 0.2200300516248938)

NT = (((1,), (1,)), ((), ()))


def dot(a, b):
    return jnp.dot(a, b, preferred_element_type=jnp.float32)


def dot_nt(a, b):
    return lax.dot_general(a, b, NT, preferred_element_type=jnp.float32)


def sigmoid(x):
    return 1.0 / (1.0 + jnp.exp(-x))


def softplus(x):
    z = jnp.exp(-jnp.abs(x))
    y = z / (2.0 + z)
    q = y * y
    series = 1.0 / 15.0
    for k in (13, 11, 9, 7, 5, 3, 1):
        series = series * q + 1.0 / k
    return jnp.maximum(x, 0.0) + 2.0 * y * series


def one_less_exp(x):
    small = 1.0 / 5040.0
    for k in (720, 120, 24, 6, 2, 1):
        small = 1.0 / k - x * small
    return jnp.where(x < 0.25, x * small, 1.0 - jnp.exp(-x))


def shift_down(rows):
    total = rows[0:1]
    out = [jnp.zeros_like(total), total]
    for s in range(1, rows.shape[0] - 1):
        total = total + rows[s : s + 1]
        out.append(total)
    return jnp.concatenate(out, axis=0)


def ray_terms(raw, step, first, last):
    slot = lax.broadcasted_iota(jnp.int32, step.shape, 0)
    live = ((slot >= first) & (slot < last)).astype(jnp.float32)
    density = softplus(raw[0])
    colour = [sigmoid(raw[c]) for c in (1, 2, 3)]
    optical = density * step * live
    before = shift_down(optical)
    blend = jnp.exp(-before) * one_less_exp(optical)
    return live, colour, optical, before, blend


def row_sum(x):
    return jnp.sum(x, axis=0, keepdims=True)


def put(ref, value):
    for j in range(ref.shape[1]):
        ref[0, j] = value[:, j * LANES : (j + 1) * LANES]


def take(ref, part=0, parts=1):
    tiles = ref.shape[1] // parts
    return jnp.concatenate([ref[0, j] for j in range(part * tiles, (part + 1) * tiles)], axis=1)


def silu(half):
    w = jnp.tanh(half) + 1.0
    hidden = half * w
    return hidden, hidden * (2.0 - w) + w


def forward_kernel(
    coords_ref, bounds_ref, step_ref, depth_ref, w_in_ref, w_mid_ref, w_out_ref, bias_ref,
    seg_ref, enc_ref, half1_ref, half2_ref, raw_ref,
    w1_ref, w2_ref, b2_ref, wide_ref, scale_ref, pos_ref,
):
    slots, rays = step_ref.shape[1], step_ref.shape[2]
    freqs = w_in_ref.shape[1] // 6

    @pl.when(pl.program_id(0) == 0)
    def _():
        wide_ref[...] = jnp.zeros_like(wide_ref)
        w_in = w_in_ref[0].astype(jnp.float32) * 0.5
        for part in range(2):
            for l in range(freqs):
                to = part * 32 + (l % 2) * 16 + (l // 2) * 3
                at = part * 3 * freqs + l * 3
                wide_ref[to : to + 3, :] = w_in[at : at + 3, :]
        half_bias = bias_ref[0] * 0.5
        upper = half_bias[0:1].astype(jnp.bfloat16).astype(jnp.float32)
        wide_ref[47:48, :] = upper
        wide_ref[63:64, :] = half_bias[0:1] - upper
        w1_ref[...] = wide_ref[...].T.astype(jnp.bfloat16)
        w2_ref[...] = (w_mid_ref[0].astype(jnp.float32) * 0.5).T.astype(jnp.bfloat16)
        b2_ref[...] = jnp.broadcast_to(half_bias[1:2], (LANES, half_bias.shape[1])).T
        row = lax.broadcasted_iota(jnp.int32, scale_ref.shape, 0)
        scale = jnp.zeros(scale_ref.shape, jnp.float32)
        for l in range(0, freqs, 2):
            scale = jnp.where(row // 3 == l // 2, 2.0 ** (l - 1), scale)
        scale_ref[...] = scale

    for c in range(3):
        p = (coords_ref[c, 0].astype(jnp.float32) + 0.5) * (1.0 / GRID)
        angle = p * math.pi
        error = ((angle - p * PI_HI) - p * PI_MID) - p * PI_LO
        pos_ref[c] = p
        pos_ref[3 + c] = error * (1.0 / math.pi)

    count = slots * rays
    coord = lax.broadcasted_iota(jnp.int32, (16, count), 0) % 3
    scale = scale_ref[...]
    rows = [
        jnp.broadcast_to(
            jnp.concatenate([pos_ref[i, s : s + 1, :] for s in range(slots)], axis=1), (16, count)
        )
        for i in range(6)
    ]
    p = jnp.where(coord == 0, rows[0], jnp.where(coord == 1, rows[1], rows[2]))
    e = jnp.where(coord == 0, rows[3], jnp.where(coord == 1, rows[4], rows[5]))
    turns = p * scale
    r = (turns - jnp.round(turns)) + e * scale
    q = r * r
    sine = SIN_COEFS[4]
    for coef in SIN_COEFS[3::-1]:
        sine = sine * q + coef
    sine = sine * r
    cosine = COS_COEFS[3]
    for coef in COS_COEFS[2::-1]:
        cosine = cosine * q + coef
    cosine = cosine * q + 1.0
    twice = sine + sine
    sin_even = twice * cosine
    cos_even = 1.0 - twice * sine
    twice = sin_even + sin_even
    sin_odd = twice * cos_even
    cos_odd = 1.0 - twice * sin_even
    enc = jnp.concatenate([sin_even, sin_odd, cos_even, cos_odd], axis=0).astype(jnp.bfloat16)
    enc_ref[0] = enc
    half = dot(w1_ref[...], enc).astype(jnp.bfloat16)
    put(half1_ref, half)
    hidden, _ = silu(half)
    b2 = jnp.concatenate([b2_ref[...]] * (count // LANES), axis=1)
    half = (dot(w2_ref[...], hidden) + b2).astype(jnp.bfloat16)
    put(half2_ref, half)
    hidden, _ = silu(half)
    raw_all = dot(w_out_ref[0], hidden)
    for s in range(slots):
        for c in range(4):
            raw_ref[0, c, s : s + 1, :] = raw_all[c : c + 1, s * rays : (s + 1) * rays]

    raw = [raw_ref[0, c] for c in range(4)]
    step = step_ref[0]
    live, colour, optical, before, blend = ray_terms(raw, step, bounds_ref[0], bounds_ref[1])
    sums = [row_sum(blend * colour[c]) for c in range(3)]
    sums.append(row_sum(blend * depth_ref[0]))
    sums.append(-row_sum(optical))
    for j in range(rays // LANES):
        for i in range(5):
            seg_ref[j, i : i + 1, :] = sums[i][:, j * LANES : (j + 1) * LANES]


def join_kernel(region_ref, seg_ref, rank_ref, target_ref, out_ref, *, loss_scale):
    regions = seg_ref.shape[0]
    rank = rank_ref[...]
    seg = [seg_ref[:, i, :] for i in range(5)]
    passing = jnp.zeros_like(rank)
    for r in range(regions):
        passing = passing + jnp.where(rank[r : r + 1] < rank, seg[4][r : r + 1], 0.0)
    light = jnp.exp(passing)
    grads = []
    weighted = jnp.zeros_like(light)
    for i in range(4):
        gain = 2.0 * loss_scale * (DEPTH_WEIGHT if i == 3 else 1.0)
        grad = gain * (row_sum(light * seg[i]) - target_ref[i : i + 1])
        grads.append(grad)
        weighted = weighted + grad * seg[i]
    terms = light * weighted
    later = jnp.zeros_like(terms)
    for r in range(regions):
        later = later + jnp.where(rank[r : r + 1] > rank, terms[r : r + 1], 0.0)
    for i in range(4):
        out_ref[:, i, :] = light * grads[i]
    out_ref[:, 4, :] = later


def backward_kernel(
    place_ref, grad_ref, bounds_ref, step_ref, depth_ref, w_mid_ref, w_out_ref,
    enc_ref, half1_ref, half2_ref, raw_ref,
    mine_ref, other_ref,
    wm_ref, wo_ref, mid_ref, in_ref, outer_ref, gr_ref, all_ref,
):
    slots, rays = step_ref.shape[1], step_ref.shape[2]

    @pl.when(pl.program_id(0) == 0)
    def _():
        wm_ref[...] = (w_mid_ref[0].astype(jnp.float32) * 0.5).astype(jnp.bfloat16)
        w_out = w_out_ref[0].astype(jnp.float32) * 0.5
        w_out = jnp.concatenate([w_out, jnp.zeros_like(w_out)], axis=0)
        wo_ref[...] = w_out.T.astype(jnp.bfloat16)
        mid_ref[...] = jnp.zeros_like(mid_ref)
        in_ref[...] = jnp.zeros_like(in_ref)
        outer_ref[...] = jnp.zeros_like(outer_ref)
        gr_ref[...] = jnp.zeros_like(gr_ref)

    raw = [raw_ref[0, c] for c in range(4)]
    step = step_ref[0]
    live, colour, optical, before, blend = ray_terms(raw, step, bounds_ref[0], bounds_ref[1])
    grad = [
        jnp.concatenate([grad_ref[j, i : i + 1, :] for j in range(rays // LANES)], axis=1)
        for i in range(5)
    ]
    usage = grad[3] * depth_ref[0]
    for c in range(3):
        usage = usage + grad[c] * colour[c]
    weighted = usage * blend
    later = row_sum(weighted) - (shift_down(weighted) + weighted)
    grad_optical = usage * jnp.exp(-(before + optical)) - later - grad[4]
    grad_raw = [grad_optical * step * live * sigmoid(raw[0])]
    for c in range(3):
        grad_raw.append(grad[c] * blend * colour[c] * (1.0 - colour[c]))
    count = slots * rays
    for s in range(slots):
        for c in range(4):
            gr_ref[c : c + 1, s * rays : (s + 1) * rays] = grad_raw[c][s : s + 1]

    gr = gr_ref[...].astype(jnp.bfloat16)
    grad_two = dot(wo_ref[...], gr).astype(jnp.bfloat16)
    hidden_two, slope_two = silu(take(half2_ref))
    d2 = grad_two * slope_two
    grad_one = dot(wm_ref[...], d2).astype(jnp.bfloat16)
    hidden, slope = silu(take(half1_ref))
    d1 = grad_one * slope
    in_ref[...] += dot_nt(enc_ref[0], d1)
    ones = jnp.ones((16, count), jnp.bfloat16)
    mid_ref[...] += dot_nt(jnp.concatenate([hidden, ones], axis=0), d2)
    outer_ref[...] += dot_nt(gr, hidden_two)

    @pl.when(pl.program_id(0) == pl.num_programs(0) - 1)
    def _():
        hid = mid_ref.shape[1]
        blank = jnp.zeros((LANES - ENC_ROWS - 24, hid), jnp.float32)
        rest = jnp.concatenate([in_ref[...], mid_ref[hid:, :], outer_ref[...], blank], axis=0)
        all_ref[:, hid:] = rest.T
        all_ref[:, :hid] = mid_ref[:hid, :].T
        chips, width = mine_ref.shape[:2]
        core = place_ref[0] % 2
        for k in range(chips):
            pair = k * 2
            mine_ref[k] = all_ref[pl.ds(pl.multiple_of((pair + core) * width, width), width), :]
            other_ref[k] = all_ref[pl.ds(pl.multiple_of((pair + 1 - core) * width, width), width), :]


def finish_kernel(parts_ref, in_ref, mid_ref, out_ref, bias_ref):
    total = parts_ref[0]
    for k in range(1, parts_ref.shape[0]):
        total = total + parts_ref[k]
    hid = mid_ref.shape[2]
    freqs = in_ref.shape[2] // 6
    mid_ref[0] = total[:, :hid]
    rest = total[:, hid:].T
    rows = []
    for part in range(2):
        for l in range(freqs):
            at = part * 32 + (l % 2) * 16 + (l // 2) * 3
            rows.append(rest[at : at + 3, :])
    in_ref[0] = jnp.concatenate(rows, axis=0).T
    out_ref[0] = rest[ENC_ROWS + 16 : ENC_ROWS + 20, :]
    bias_ref[0, 0:1, :] = rest[47:48, :]
    bias_ref[0, 1:2, :] = rest[ENC_ROWS : ENC_ROWS + 1, :]


def whole(shape):
    return pl.BlockSpec(shape, lambda *_: (0,) * len(shape))


def on_device(
    grid_coords, segment_bounds, depth_rank, step_length, sample_depth,
    target_pixels, weight_in, weight_mid, weight_out, bias_hidden,
):
    f32, bf16 = jnp.float32, jnp.bfloat16
    _, slots, ray_count = step_length.shape
    regions = depth_rank.shape[1]
    enc, hid = weight_in.shape[1:]
    ways = lax.axis_size("rays")
    loss_scale = 1.0 / math.sqrt(ray_count * ways)
    rays = 512
    tiles = ray_count // rays
    chunk = rays // LANES
    arbitrary = pltpu.CompilerParams(dimension_semantics=("arbitrary",))

    small = pltpu.CompilerParams(vmem_limit_bytes=4 << 20)
    lp = pltpu.CompilerParams(dimension_semantics=("arbitrary",))

    ray_specs = [
        pl.BlockSpec((2, 1, rays), lambda t: (0, 0, t)),
        pl.BlockSpec((1, slots, rays), lambda t: (0, 0, t)),
        pl.BlockSpec((1, slots, rays), lambda t: (0, 0, t)),
    ]
    seg_spec = pl.BlockSpec((chunk, 8, LANES), lambda t: (t, 0, 0))
    save_specs = (
        [pl.BlockSpec((1, ENC_ROWS, slots * rays), lambda t: (t, 0, 0))]
        + [pl.BlockSpec((1, slots * chunk, hid, LANES), lambda t: (t, 0, 0, 0))] * 2
        + [pl.BlockSpec((1, 4, slots, rays), lambda t: (t, 0, 0, 0))]
    )
    save_shapes = (
        [jax.ShapeDtypeStruct((tiles, ENC_ROWS, slots * rays), bf16)]
        + [jax.ShapeDtypeStruct((tiles, slots * chunk, hid, LANES), bf16)] * 2
        + [jax.ShapeDtypeStruct((tiles, 4, slots, rays), f32)]
    )

    outs = pl.pallas_call(
        forward_kernel,
        grid=(tiles,),
        in_specs=[pl.BlockSpec((3, 1, slots, rays), lambda t: (0, 0, 0, t))]
        + ray_specs
        + [whole(weight_in.shape), whole(weight_mid.shape), whole(weight_out.shape), whole(bias_hidden.shape)],
        out_specs=[seg_spec] + save_specs,
        out_shape=[jax.ShapeDtypeStruct((ray_count // LANES, 8, LANES), f32)] + save_shapes,
        scratch_shapes=[
            pltpu.VMEM((hid, ENC_ROWS), bf16),
            pltpu.VMEM((hid, hid), bf16),
            pltpu.VMEM((hid, LANES), f32),
            pltpu.VMEM((ENC_ROWS, hid), f32),
            pltpu.VMEM((16, slots * rays), f32),
            pltpu.VMEM((6, slots, rays), f32),
        ],
        compiler_params=arbitrary,
        name="forward",
    )(grid_coords, segment_bounds, step_length, sample_depth, weight_in, weight_mid, weight_out, bias_hidden)
    segment, saved = outs[0], outs[1:]

    segments = lax.all_to_all(segment, "region", 0, 0, tiled=True)
    own = ray_count // regions
    position = lax.axis_index("region").astype(jnp.int32).reshape(1)
    joined = pl.pallas_call(
        functools.partial(join_kernel, loss_scale=loss_scale),
        grid_spec=pltpu.PrefetchScalarGridSpec(
            num_scalar_prefetch=1,
            grid=(1,),
            in_specs=[
                pl.BlockSpec((regions, 8, own), lambda t, at: (0, 0, 0)),
                pl.BlockSpec((regions, own), lambda t, at: (0, at[0])),
                pl.BlockSpec((4, own), lambda t, at: (0, at[0])),
            ],
            out_specs=pl.BlockSpec((regions, 8, own), lambda t, at: (0, 0, 0)),
        ),
        out_shape=jax.ShapeDtypeStruct((regions, 8, own), f32),
        compiler_params=arbitrary,
        name="join",
    )(position, segments, depth_rank.T, target_pixels)
    segment_grad = lax.all_to_all(joined, "region", 0, 0, tiled=True)

    width = hid // ways
    chips = ways // 2

    def at(spec):
        return pl.BlockSpec(spec.block_shape, lambda t, _: spec.index_map(t))

    place = lax.axis_index("rays").astype(jnp.int32).reshape(1)
    mine, other = pl.pallas_call(
        backward_kernel,
        grid_spec=pltpu.PrefetchScalarGridSpec(
            num_scalar_prefetch=1,
            grid=(tiles,),
            in_specs=[
                at(spec)
                for spec in [seg_spec] + ray_specs + [whole(weight_mid.shape), whole(weight_out.shape)] + save_specs
            ],
            out_specs=[whole((chips, width, hid + LANES))] * 2,
            scratch_shapes=[
                pltpu.VMEM((hid, hid), bf16),
                pltpu.VMEM((hid, 8), bf16),
                pltpu.VMEM((hid + 16, hid), f32),
                pltpu.VMEM((ENC_ROWS, hid), f32),
                pltpu.VMEM((8, hid), f32),
                pltpu.VMEM((8, slots * rays), f32),
                pltpu.VMEM((hid, hid + LANES), f32),
            ],
        ),
        out_shape=[jax.ShapeDtypeStruct((chips, width, hid + LANES), f32)] * 2,
        compiler_params=lp,
        name="backward",
    )(place, segment_grad, segment_bounds, step_length, sample_depth, weight_mid, weight_out, *saved)

    pairs = mine + lax.ppermute(other, "rays", [(i, i ^ 1) for i in range(ways)])
    rings = [list(range(core, ways, 2)) for core in range(2)]
    parts = lax.all_to_all(pairs, "rays", 0, 0, tiled=True, axis_index_groups=rings)
    grad_in, grad_mid, grad_out, grad_bias = pl.pallas_call(
        finish_kernel,
        out_shape=[
            jax.ShapeDtypeStruct(shape, f32)
            for shape in ((1, width, enc), (1, width, hid), (1, 4, width), (1, 2, width))
        ],
        compiler_params=small,
        name="finish",
    )(parts)
    return jnp.swapaxes(grad_in, 1, 2), jnp.swapaxes(grad_mid, 1, 2), grad_out, grad_bias


def solution(mesh):
    placed = (
        P(None, "region", None, "rays"),
        P(None, "region", "rays"),
        P("rays", None),
        P("region", None, "rays"),
        P("region", None, "rays"),
        P(None, "rays"),
        P("region", None, None),
        P("region", None, None),
        P("region", None, None),
        P("region", None, None),
    )
    return jax.shard_map(
        on_device,
        mesh=mesh,
        in_specs=placed,
        out_specs=(P("region", None, "rays"),) * 4,
        check_vma=False,
    )
```

```python
import functools
import math

import jax
import jax.numpy as jnp
from jax import lax
from jax.experimental import pallas as pl
from jax.experimental.pallas import tpu as pltpu
from jax.sharding import PartitionSpec as P

GRID = 4096
LANES = 128
DEPTH_WEIGHT = 0.1
ENC_ROWS = 64

PI_HI = 3.140625
PI_MID = 9.67502593994140625e-4
PI_LO = 1.509957990978376432e-7

SIN_COEFS = (3.1415925798055784, -5.167706866167917, 2.5500311935189344, -0.5980441939097795, 0.07721838615261653)
COS_COEFS = (-4.934795324080539, 4.058447258699471, -1.332068065877436, 0.2200300516248938)

NT = (((1,), (1,)), ((), ()))


def dot(a, b):
    return jnp.dot(a, b, preferred_element_type=jnp.float32)


def dot_nt(a, b):
    return lax.dot_general(a, b, NT, preferred_element_type=jnp.float32)


def sigmoid(x):
    return 1.0 / (1.0 + jnp.exp(-x))


def softplus(x):
    z = jnp.exp(-jnp.abs(x))
    y = z / (2.0 + z)
    q = y * y
    series = 1.0 / 15.0
    for k in (13, 11, 9, 7, 5, 3, 1):
        series = series * q + 1.0 / k
    return jnp.maximum(x, 0.0) + 2.0 * y * series


def one_less_exp(x):
    small = 1.0 / 5040.0
    for k in (720, 120, 24, 6, 2, 1):
        small = 1.0 / k - x * small
    return jnp.where(x < 0.25, x * small, 1.0 - jnp.exp(-x))


def shift_down(rows):
    total = rows[0:1]
    out = [jnp.zeros_like(total), total]
    for s in range(1, rows.shape[0] - 1):
        total = total + rows[s : s + 1]
        out.append(total)
    return jnp.concatenate(out, axis=0)


def ray_terms(raw, step, first, last):
    slot = lax.broadcasted_iota(jnp.int32, step.shape, 0)
    live = ((slot >= first) & (slot < last)).astype(jnp.float32)
    density = softplus(raw[0])
    colour = [sigmoid(raw[c]) for c in (1, 2, 3)]
    optical = density * step * live
    before = shift_down(optical)
    blend = jnp.exp(-before) * one_less_exp(optical)
    return live, colour, optical, before, blend


def row_sum(x):
    return jnp.sum(x, axis=0, keepdims=True)


def put(ref, value):
    for j in range(ref.shape[1]):
        ref[0, j] = value[:, j * LANES : (j + 1) * LANES]


def take(ref, part=0, parts=1):
    tiles = ref.shape[1] // parts
    return jnp.concatenate([ref[0, j] for j in range(part * tiles, (part + 1) * tiles)], axis=1)


def silu(half):
    w = jnp.tanh(half) + 1.0
    hidden = half * w
    return hidden, hidden * (2.0 - w) + w


def forward_kernel(
    coords_ref, bounds_ref, step_ref, depth_ref, w_in_ref, w_mid_ref, w_out_ref, bias_ref,
    seg_ref, enc_ref, half1_ref, half2_ref, raw_ref,
    w1_ref, w2_ref, b2_ref, wide_ref, scale_ref, pos_ref,
):
    slots, rays = step_ref.shape[1], step_ref.shape[2]
    freqs = w_in_ref.shape[1] // 6

    @pl.when(pl.program_id(0) == 0)
    def _():
        wide_ref[...] = jnp.zeros_like(wide_ref)
        w_in = w_in_ref[0].astype(jnp.float32) * 0.5
        for part in range(2):
            for l in range(freqs):
                to = part * 32 + (l % 2) * 16 + (l // 2) * 3
                at = part * 3 * freqs + l * 3
                wide_ref[to : to + 3, :] = w_in[at : at + 3, :]
        half_bias = bias_ref[0] * 0.5
        upper = half_bias[0:1].astype(jnp.bfloat16).astype(jnp.float32)
        wide_ref[47:48, :] = upper
        wide_ref[63:64, :] = half_bias[0:1] - upper
        w1_ref[...] = wide_ref[...].T.astype(jnp.bfloat16)
        w2_ref[...] = (w_mid_ref[0].astype(jnp.float32) * 0.5).T.astype(jnp.bfloat16)
        b2_ref[...] = jnp.broadcast_to(half_bias[1:2], (LANES, half_bias.shape[1])).T
        row = lax.broadcasted_iota(jnp.int32, scale_ref.shape, 0)
        scale = jnp.zeros(scale_ref.shape, jnp.float32)
        for l in range(0, freqs, 2):
            scale = jnp.where(row // 3 == l // 2, 2.0 ** (l - 1), scale)
        scale_ref[...] = scale

    for c in range(3):
        p = (coords_ref[c, 0].astype(jnp.float32) + 0.5) * (1.0 / GRID)
        angle = p * math.pi
        error = ((angle - p * PI_HI) - p * PI_MID) - p * PI_LO
        pos_ref[c] = p
        pos_ref[3 + c] = error * (1.0 / math.pi)

    count = slots * rays
    coord = lax.broadcasted_iota(jnp.int32, (16, count), 0) % 3
    scale = scale_ref[...]
    rows = [
        jnp.broadcast_to(
            jnp.concatenate([pos_ref[i, s : s + 1, :] for s in range(slots)], axis=1), (16, count)
        )
        for i in range(6)
    ]
    p = jnp.where(coord == 0, rows[0], jnp.where(coord == 1, rows[1], rows[2]))
    e = jnp.where(coord == 0, rows[3], jnp.where(coord == 1, rows[4], rows[5]))
    turns = p * scale
    r = (turns - jnp.round(turns)) + e * scale
    q = r * r
    sine = SIN_COEFS[4]
    for coef in SIN_COEFS[3::-1]:
        sine = sine * q + coef
    sine = sine * r
    cosine = COS_COEFS[3]
    for coef in COS_COEFS[2::-1]:
        cosine = cosine * q + coef
    cosine = cosine * q + 1.0
    twice = sine + sine
    sin_even = twice * cosine
    cos_even = 1.0 - twice * sine
    twice = sin_even + sin_even
    sin_odd = twice * cos_even
    cos_odd = 1.0 - twice * sin_even
    enc = jnp.concatenate([sin_even, sin_odd, cos_even, cos_odd], axis=0).astype(jnp.bfloat16)
    enc_ref[0] = enc
    half = dot(w1_ref[...], enc).astype(jnp.bfloat16)
    put(half1_ref, half)
    hidden, _ = silu(half)
    b2 = jnp.concatenate([b2_ref[...]] * (count // LANES), axis=1)
    half = (dot(w2_ref[...], hidden) + b2).astype(jnp.bfloat16)
    put(half2_ref, half)
    hidden, _ = silu(half)
    raw_all = dot(w_out_ref[0], hidden)
    for s in range(slots):
        for c in range(4):
            raw_ref[0, c, s : s + 1, :] = raw_all[c : c + 1, s * rays : (s + 1) * rays]

    raw = [raw_ref[0, c] for c in range(4)]
    step = step_ref[0]
    live, colour, optical, before, blend = ray_terms(raw, step, bounds_ref[0], bounds_ref[1])
    sums = [row_sum(blend * colour[c]) for c in range(3)]
    sums.append(row_sum(blend * depth_ref[0]))
    sums.append(-row_sum(optical))
    for j in range(rays // LANES):
        for i in range(5):
            seg_ref[j, i : i + 1, :] = sums[i][:, j * LANES : (j + 1) * LANES]


def join_kernel(seg_ref, rank_ref, target_ref, out_ref, *, loss_scale):
    regions = seg_ref.shape[0]
    rank = rank_ref[...]
    seg = [seg_ref[:, i, :] for i in range(5)]
    passing = jnp.zeros_like(rank)
    for r in range(regions):
        passing = passing + jnp.where(rank[r : r + 1] < rank, seg[4][r : r + 1], 0.0)
    light = jnp.exp(passing)
    grads = []
    weighted = jnp.zeros_like(light)
    for i in range(4):
        gain = 2.0 * loss_scale * (DEPTH_WEIGHT if i == 3 else 1.0)
        grad = gain * (row_sum(light * seg[i]) - target_ref[i : i + 1])
        grads.append(grad)
        weighted = weighted + grad * seg[i]
    terms = light * weighted
    later = jnp.zeros_like(terms)
    for r in range(regions):
        later = later + jnp.where(rank[r : r + 1] > rank, terms[r : r + 1], 0.0)
    for i in range(4):
        out_ref[:, i, :] = light * grads[i]
    out_ref[:, 4, :] = later


def backward_kernel(
    place_ref, grad_ref, bounds_ref, step_ref, depth_ref, w_mid_ref, w_out_ref,
    enc_ref, half1_ref, half2_ref, raw_ref,
    mine_ref, other_ref,
    wm_ref, wo_ref, mid_ref, in_ref, outer_ref, gr_ref, all_ref,
):
    slots, rays = step_ref.shape[1], step_ref.shape[2]

    @pl.when(pl.program_id(0) == 0)
    def _():
        wm_ref[...] = (w_mid_ref[0].astype(jnp.float32) * 0.5).astype(jnp.bfloat16)
        w_out = w_out_ref[0].astype(jnp.float32) * 0.5
        w_out = jnp.concatenate([w_out, jnp.zeros_like(w_out)], axis=0)
        wo_ref[...] = w_out.T.astype(jnp.bfloat16)
        mid_ref[...] = jnp.zeros_like(mid_ref)
        in_ref[...] = jnp.zeros_like(in_ref)
        outer_ref[...] = jnp.zeros_like(outer_ref)
        gr_ref[...] = jnp.zeros_like(gr_ref)

    raw = [raw_ref[0, c] for c in range(4)]
    step = step_ref[0]
    live, colour, optical, before, blend = ray_terms(raw, step, bounds_ref[0], bounds_ref[1])
    grad = [
        jnp.concatenate([grad_ref[j, i : i + 1, :] for j in range(rays // LANES)], axis=1)
        for i in range(5)
    ]
    usage = grad[3] * depth_ref[0]
    for c in range(3):
        usage = usage + grad[c] * colour[c]
    weighted = usage * blend
    later = row_sum(weighted) - (shift_down(weighted) + weighted)
    grad_optical = usage * jnp.exp(-(before + optical)) - later - grad[4]
    grad_raw = [grad_optical * step * live * sigmoid(raw[0])]
    for c in range(3):
        grad_raw.append(grad[c] * blend * colour[c] * (1.0 - colour[c]))
    count = slots * rays
    for s in range(slots):
        for c in range(4):
            gr_ref[c : c + 1, s * rays : (s + 1) * rays] = grad_raw[c][s : s + 1]

    gr = gr_ref[...].astype(jnp.bfloat16)
    grad_two = dot(wo_ref[...], gr).astype(jnp.bfloat16)
    hidden_two, slope_two = silu(take(half2_ref))
    d2 = grad_two * slope_two
    grad_one = dot(wm_ref[...], d2).astype(jnp.bfloat16)
    hidden, slope = silu(take(half1_ref))
    d1 = grad_one * slope
    in_ref[...] += dot_nt(enc_ref[0], d1)
    ones = jnp.ones((16, count), jnp.bfloat16)
    mid_ref[...] += dot_nt(jnp.concatenate([hidden, ones], axis=0), d2)
    outer_ref[...] += dot_nt(gr, hidden_two)

    @pl.when(pl.program_id(0) == pl.num_programs(0) - 1)
    def _():
        hid = mid_ref.shape[1]
        blank = jnp.zeros((LANES - ENC_ROWS - 24, hid), jnp.float32)
        rest = jnp.concatenate([in_ref[...], mid_ref[hid:, :], outer_ref[...], blank], axis=0)
        all_ref[:, hid:] = rest.T
        all_ref[:, :hid] = mid_ref[:hid, :].T
        chips, width = mine_ref.shape[:2]
        chip = place_ref[0] // 2
        core = place_ref[0] % 2
        for k in range(chips):
            pair = lax.rem(chip + k, chips) * 2
            mine_ref[k] = all_ref[pl.ds(pl.multiple_of((pair + core) * width, width), width), :]
            other_ref[k] = all_ref[pl.ds(pl.multiple_of((pair + 1 - core) * width, width), width), :]


def finish_kernel(own_ref, one_ref, two_ref, three_ref, in_ref, mid_ref, out_ref, bias_ref):
    total = (own_ref[...] + one_ref[...]) + (two_ref[...] + three_ref[...])
    hid = mid_ref.shape[2]
    freqs = in_ref.shape[2] // 6
    mid_ref[0] = total[:, :hid]
    rest = total[:, hid:].T
    rows = []
    for part in range(2):
        for l in range(freqs):
            at = part * 32 + (l % 2) * 16 + (l // 2) * 3
            rows.append(rest[at : at + 3, :])
    in_ref[0] = jnp.concatenate(rows, axis=0).T
    out_ref[0] = rest[ENC_ROWS + 16 : ENC_ROWS + 20, :]
    bias_ref[0, 0:1, :] = rest[47:48, :]
    bias_ref[0, 1:2, :] = rest[ENC_ROWS : ENC_ROWS + 1, :]


def whole(shape):
    return pl.BlockSpec(shape, lambda *_: (0,) * len(shape))


def on_device(
    grid_coords, segment_bounds, depth_rank, step_length, sample_depth,
    target_pixels, weight_in, weight_mid, weight_out, bias_hidden,
):
    f32, bf16 = jnp.float32, jnp.bfloat16
    _, slots, ray_count = step_length.shape
    regions = depth_rank.shape[1]
    enc, hid = weight_in.shape[1:]
    ways = lax.axis_size("rays")
    loss_scale = 1.0 / math.sqrt(ray_count * ways)
    rays = 512
    tiles = ray_count // rays
    chunk = rays // LANES
    arbitrary = pltpu.CompilerParams(dimension_semantics=("arbitrary",))

    small = pltpu.CompilerParams(vmem_limit_bytes=4 << 20)
    lp = pltpu.CompilerParams(dimension_semantics=("arbitrary",))

    ray_specs = [
        pl.BlockSpec((2, 1, rays), lambda t: (0, 0, t)),
        pl.BlockSpec((1, slots, rays), lambda t: (0, 0, t)),
        pl.BlockSpec((1, slots, rays), lambda t: (0, 0, t)),
    ]
    seg_spec = pl.BlockSpec((chunk, 8, LANES), lambda t: (t, 0, 0))
    save_specs = (
        [pl.BlockSpec((1, ENC_ROWS, slots * rays), lambda t: (t, 0, 0))]
        + [pl.BlockSpec((1, slots * chunk, hid, LANES), lambda t: (t, 0, 0, 0))] * 2
        + [pl.BlockSpec((1, 4, slots, rays), lambda t: (t, 0, 0, 0))]
    )
    save_shapes = (
        [jax.ShapeDtypeStruct((tiles, ENC_ROWS, slots * rays), bf16)]
        + [jax.ShapeDtypeStruct((tiles, slots * chunk, hid, LANES), bf16)] * 2
        + [jax.ShapeDtypeStruct((tiles, 4, slots, rays), f32)]
    )

    outs = pl.pallas_call(
        forward_kernel,
        grid=(tiles,),
        in_specs=[pl.BlockSpec((3, 1, slots, rays), lambda t: (0, 0, 0, t))]
        + ray_specs
        + [whole(weight_in.shape), whole(weight_mid.shape), whole(weight_out.shape), whole(bias_hidden.shape)],
        out_specs=[seg_spec] + save_specs,
        out_shape=[jax.ShapeDtypeStruct((ray_count // LANES, 8, LANES), f32)] + save_shapes,
        scratch_shapes=[
            pltpu.VMEM((hid, ENC_ROWS), bf16),
            pltpu.VMEM((hid, hid), bf16),
            pltpu.VMEM((hid, LANES), f32),
            pltpu.VMEM((ENC_ROWS, hid), f32),
            pltpu.VMEM((16, slots * rays), f32),
            pltpu.VMEM((6, slots, rays), f32),
        ],
        compiler_params=arbitrary,
        name="forward",
    )(grid_coords, segment_bounds, step_length, sample_depth, weight_in, weight_mid, weight_out, bias_hidden)
    segment, saved = outs[0], outs[1:]

    segments = lax.all_to_all(segment, "region", 0, 0, tiled=True)
    own = ray_count // regions
    start = lax.axis_index("region") * own
    joined = pl.pallas_call(
        functools.partial(join_kernel, loss_scale=loss_scale),
        in_specs=[pl.BlockSpec(memory_space=pltpu.VMEM)] * 3,
        out_specs=pl.BlockSpec(memory_space=pltpu.VMEM),
        out_shape=jax.ShapeDtypeStruct((regions, 8, own), f32),
        compiler_params=small,
        name="join",
    )(
        segments,
        lax.dynamic_slice_in_dim(depth_rank.T, start, own, axis=1),
        lax.dynamic_slice_in_dim(target_pixels, start, own, axis=1),
    )
    segment_grad = lax.all_to_all(joined, "region", 0, 0, tiled=True)

    width = hid // ways
    chips = ways // 2

    def at(spec):
        return pl.BlockSpec(spec.block_shape, lambda t, _: spec.index_map(t))

    place = lax.axis_index("rays").astype(jnp.int32).reshape(1)
    mine, other = pl.pallas_call(
        backward_kernel,
        grid_spec=pltpu.PrefetchScalarGridSpec(
            num_scalar_prefetch=1,
            grid=(tiles,),
            in_specs=[
                at(spec)
                for spec in [seg_spec] + ray_specs + [whole(weight_mid.shape), whole(weight_out.shape)] + save_specs
            ],
            out_specs=[whole((chips, width, hid + LANES))] * 2,
            scratch_shapes=[
                pltpu.VMEM((hid, hid), bf16),
                pltpu.VMEM((hid, 8), bf16),
                pltpu.VMEM((hid + 16, hid), f32),
                pltpu.VMEM((ENC_ROWS, hid), f32),
                pltpu.VMEM((8, hid), f32),
                pltpu.VMEM((8, slots * rays), f32),
                pltpu.VMEM((hid, hid + LANES), f32),
            ],
        ),
        out_shape=[jax.ShapeDtypeStruct((chips, width, hid + LANES), f32)] * 2,
        compiler_params=lp,
        name="backward",
    )(place, segment_grad, segment_bounds, step_length, sample_depth, weight_mid, weight_out, *saved)

    arrived = lax.ppermute(other, "rays", [(i, i ^ 1) for i in range(ways)])
    pairs = [mine[k] + arrived[k] for k in range(chips)]
    parts = [pairs[0]] + [
        lax.ppermute(pairs[k], "rays", [(i, (i + 2 * k) % ways) for i in range(ways)])
        for k in range(1, chips)
    ]
    grad_in, grad_mid, grad_out, grad_bias = pl.pallas_call(
        finish_kernel,
        out_shape=[
            jax.ShapeDtypeStruct(shape, f32)
            for shape in ((1, width, enc), (1, width, hid), (1, 4, width), (1, 2, width))
        ],
        compiler_params=small,
        name="finish",
    )(*parts)
    return jnp.swapaxes(grad_in, 1, 2), jnp.swapaxes(grad_mid, 1, 2), grad_out, grad_bias


def solution(mesh):
    placed = (
        P(None, "region", None, "rays"),
        P(None, "region", "rays"),
        P("rays", None),
        P("region", None, "rays"),
        P("region", None, "rays"),
        P(None, "rays"),
        P("region", None, None),
        P("region", None, None),
        P("region", None, None),
        P("region", None, None),
    )
    return jax.shard_map(
        on_device,
        mesh=mesh,
        in_specs=placed,
        out_specs=(P("region", None, "rays"),) * 4,
        check_vma=False,
    )
```
